512 devices in a mesh: slab: 32 (over z, y_lo), face: 16 (over y_hi, x, core).
Axes of the slice: x: 4, y: 4 (y_hi: 2, y_lo: 2; y = y_hi * 2 + y_lo), z: 16, core: 2. Of those that a mesh axis runs over, the one named last changes fastest.
Arguments:
- rhs: bfloat16 [4, 32, 128, 16384], P(None, 'slab', None, 'face'), may hold values from -6 to 6
- inflow: bfloat16 [32, 128, 4096], P('slab', None, 'face'), may hold values from -6 to 6
- diag_tiles: bfloat16 [32, 128, 128, 128], P('slab', 'face')
- off_tiles: bfloat16 [32, 128, 4, 128, 128], P('slab', 'face'), may hold values from -0.5 to 0.5
- cols: int32 [32, 128, 4], P('slab', 'face'), may hold values from 0 to 127, as said below
- inverse_tiles: bfloat16 [32, 128, 128, 128], P('slab', 'face')
- coupling: bfloat16 [32, 32, 128, 128], P('slab', 'face'), may hold values from -1 to 1
- iface: int32 [32], P('face'), may hold values from 0 to 7, as said below
Outputs:
- solution: bfloat16 [4, 32, 128, 16384], P(None, 'slab', None, 'face')
The draws below stay inside these ranges and needn't reach their ends.
Inputs may be any that keep to these rules, and one draw needn't show every extreme that they name: `cols`: each column index lies within 2 tile rows of the block of 8 tile rows that holds its row; a block's first tile row reaches the tile row 2 before the block and its last reaches the tile row 2 after the block, wherever the slab has them. The 2 entries of one block of iface are distinct.
All inputs are finite; a program needn't handle non-finite values.
Results may differ from the reference program's by a relative error of at most 0.01.
Values may be sent and summed in bfloat16 or wider, within the bound.
A program may use at most 64 MiB of HBM per device.

```python
import jax
import jax.numpy as jnp
from jax import lax

TILE = 128
SRC = 128
TILES_DEV = 8
NEIGH = 4
HALO_T = 2
IF_T = 2
TICKS = 4
SLABS = 32
TILES_SLAB = 128
ROWS_SLAB = 16384
IF_SLAB = 32


def draw_diag_tiles(key, part):
    noise_key = jax.random.fold_in(key, 11)
    shape = (SLABS, TILES_SLAB, TILE, TILE)
    noise = 0.08 * jax.random.normal(noise_key, shape, jnp.float32)
    level = 4.0 * jnp.ones((SLABS, TILES_SLAB, 1, 1), jnp.float32)
    return (level * jnp.eye(TILE, dtype=jnp.float32) + noise).astype(jnp.bfloat16)


def draw_inverse_tiles(key, part):
    noise_key = jax.random.fold_in(key, 13)
    shape = (SLABS, TILES_SLAB, TILE, TILE)
    noise = 0.006 * jax.random.normal(noise_key, shape, jnp.float32)
    level = 0.2 * jnp.ones((SLABS, TILES_SLAB, 1, 1), jnp.float32)
    return (level * jnp.eye(TILE, dtype=jnp.float32) + noise).astype(jnp.bfloat16)


def draw_cols(key, part):
    rows = jnp.arange(TILES_SLAB, dtype=jnp.int32)
    start = rows // TILES_DEV * TILES_DEV - HALO_T
    span = TILES_DEV + 2 * HALO_T
    picks = jax.random.randint(jax.random.fold_in(key, 21), (SLABS, TILES_SLAB, NEIGH), 0, span, dtype=jnp.int32)
    local = rows % TILES_DEV
    first = jnp.where(local == 0, 0, jnp.where(local == TILES_DEV - 1, span - 1, picks[:, :, 0]))
    picks = picks.at[:, :, 0].set(first.astype(jnp.int32))
    return jnp.clip(start[None, :, None] + picks, 0, TILES_SLAB - 1).astype(jnp.int32)


def draw_iface(key, part):
    blocks = IF_SLAB // IF_T
    keys = jax.random.split(jax.random.fold_in(key, 31), blocks)

    def one_block(block_key):
        return jax.random.permutation(block_key, TILES_DEV).astype(jnp.int32)
    orders = jax.vmap(one_block)(keys)
    offset = orders[:, :1] + (jnp.arange(blocks, dtype=jnp.int32) % 2)[:, None]
    rolled = (orders - offset) % TILES_DEV
    return rolled[:, :IF_T].reshape(-1).astype(jnp.int32)


def block_scale(key, shape, cuts, least, high):
    factor_of = 1.0
    for position, blocks in cuts:
        draws = jax.random.uniform(jax.random.fold_in(jax.random.fold_in(key, 6), position), (blocks,), jnp.float32, least / len(cuts), high / len(cuts))
        factor_of = factor_of * jnp.repeat(jnp.exp(draws), shape[position] // blocks).reshape((-1,) + (1,) * (len(shape) - 1 - position))
    return factor_of


def bell_draw(own_key, extent, spread, limit, cuts=(), kind=jnp.bfloat16):
    factor_of = block_scale(own_key, extent, cuts, -0.22, 0.18) if cuts else 1.0
    entries = jax.random.normal(own_key, extent, jnp.float32) * spread * factor_of
    return jnp.minimum(jnp.maximum(entries, -limit), limit).astype(kind)


def setup_inputs(seed: int = 0) -> dict:
    arg_keys = jax.random.split(jax.random.key(seed), 9)
    rhs = bell_draw(arg_keys[0], (TICKS, SLABS, SRC, ROWS_SLAB), 1.0, 6.0, ((1, 32), (3, 16)))
    inflow = bell_draw(arg_keys[1], (SLABS, SRC, IF_SLAB * TILE), 1.0, 6.0, ((0, 32), (2, 16)))
    diag_tiles = draw_diag_tiles(jax.random.fold_in(arg_keys[8], 71), 0)
    off_tiles = bell_draw(arg_keys[3], (SLABS, TILES_SLAB, NEIGH, TILE, TILE), 0.08, 0.5, ((0, 32), (1, 16)))
    cols = draw_cols(jax.random.fold_in(arg_keys[8], 71), 0)
    inverse_tiles = draw_inverse_tiles(jax.random.fold_in(arg_keys[8], 71), 0)
    coupling = bell_draw(arg_keys[6], (SLABS, IF_SLAB, TILE, TILE), (TILE // 4) ** -0.5, 1.0, ((0, 32), (1, 16)))
    iface = draw_iface(jax.random.fold_in(arg_keys[8], 71), 0)
    return dict(rhs=rhs, inflow=inflow, diag_tiles=diag_tiles, off_tiles=off_tiles, cols=cols, inverse_tiles=inverse_tiles, coupling=coupling, iface=iface)


def tile_apply(tiles, values):
    return jnp.einsum("rij,srj->sri", tiles.astype(jnp.float32), values.astype(jnp.float32))


def slab_tick(rhs_slab, incoming, diag_slab, off_slab, cols_slab, inverse_slab, coupling_slab, iface):
    count = diag_slab.shape[0]
    width = diag_slab.shape[1]
    sources = rhs_slab.shape[0]
    inbound = incoming.reshape(sources, -1, width).astype(jnp.float32)
    coupled = jnp.einsum("qij,sqj->sqi", coupling_slab.astype(jnp.float32), inbound)
    targets = ((jnp.arange(IF_SLAB, dtype=jnp.int32) // IF_T) * TILES_DEV + iface).astype(jnp.int32)
    right = rhs_slab.reshape(sources, count, width).astype(jnp.float32)
    right = right.at[:, targets].add(-coupled)
    right = right.astype(jnp.bfloat16)
    field = tile_apply(inverse_slab, right).astype(jnp.bfloat16)
    for sweep in range(2):
        gathered = field[:, cols_slab]
        product = tile_apply(diag_slab, field) + jnp.einsum("rkij,srkj->sri", off_slab.astype(jnp.float32), gathered.astype(jnp.float32))
        correction = (right.astype(jnp.float32) - product).astype(jnp.bfloat16)
        field = (field.astype(jnp.float32) + tile_apply(inverse_slab, correction)).astype(jnp.bfloat16)
    sent = field[:, targets].reshape(sources, -1)
    return field.reshape(sources, count * width), sent


def reference(rhs, inflow, diag_tiles, off_tiles, cols, inverse_tiles, coupling, iface):
    incoming = inflow
    results = []
    for tick in range(TICKS):
        def one_slab(pieces):
            return slab_tick(pieces[0], pieces[1], pieces[2], pieces[3], pieces[4], pieces[5], pieces[6], iface)

        fields, sent = lax.map(one_slab, (rhs[tick], incoming, diag_tiles, off_tiles, cols, inverse_tiles, coupling))
        results.append(fields)
        incoming = jnp.concatenate([jnp.zeros_like(sent[:1]), sent[:-1]], axis=0)
    return jnp.stack(results)
```

```python
import functools

import jax
import jax.numpy as jnp
from jax import lax
from jax.experimental import pallas as pl
from jax.experimental.pallas import tpu as pltpu
from jax.sharding import PartitionSpec as P

HALO = 2
MESH = pl.DeviceIdType.MESH
BF16 = jnp.bfloat16
F32 = jnp.float32


def mm(u, w):
    return lax.dot_general(u, w, (((1,), (1,)), ((), ())), preferred_element_type=F32)


def kernel(S, FN, T, N, K, Q, W, *refs):
    refs = list(refs)
    take = lambda n: [refs.pop(0) for _ in range(n)]
    cols, iface, rhs, inflow, diag, off, inv, coup = take(8)
    (out,) = take(1)
    rhs_v, diag_v, off_v, inv_v, coup_v, out_v, sent = take(7)
    incs = take(T)
    rights = take(T)
    fields = take(2 * T)
    ld, st, hs, hr, ssem, rsem = take(6)

    s = lax.axis_index("slab")
    f = lax.axis_index("face")
    has_l, has_r = f > 0, f < FN - 1
    has_p, has_n = s > 0, s < S - 1
    left = (s, jnp.maximum(f - 1, 0))
    right = (s, jnp.minimum(f + 1, FN - 1))
    prev = (jnp.maximum(s - 1, 0), f)
    nxt = (jnp.minimum(s + 1, S - 1), f)

    barrier = pltpu.get_barrier_semaphore()
    for there, who in ((has_l, left), (has_r, right), (has_p, prev), (has_n, nxt)):
        @pl.when(there)
        def _(who=who):
            pl.semaphore_signal(barrier, inc=1, device_id=who, device_id_type=MESH)

    loads = [pltpu.make_async_copy(inflow.at[0, :, q * W:(q + 1) * W], incs[0].at[q], ld.at[q]) for q in range(Q)]
    loads += [
        pltpu.make_async_copy(coup.at[0], coup_v, ld.at[Q]),
        pltpu.make_async_copy(rhs.at[0, 0], rhs_v.at[0], ld.at[Q + 1]),
        pltpu.make_async_copy(inv.at[0], inv_v, ld.at[Q + 2]),
        pltpu.make_async_copy(diag.at[0], diag_v, ld.at[Q + 3]),
        pltpu.make_async_copy(off.at[0], off_v, ld.at[Q + 4]),
    ]
    loads += [pltpu.make_async_copy(rhs.at[t, 0], rhs_v.at[t], ld.at[Q + 4 + t]) for t in range(1, T)]
    for c in loads:
        c.start()

    base = f * N - HALO

    def col(r, k):
        return jnp.clip(cols[k, r] - base, 0, N + 2 * HALO - 1)

    local = [[col(r, k) for k in range(K)] for r in range(N)]
    e = [iface[q] for q in range(Q)]

    zero_halo = jnp.zeros((HALO,) + fields[0].shape[1:], BF16)
    for b in fields:
        @pl.when(f == 0)
        def _(b=b):
            b[0:HALO] = zero_halo

        @pl.when(f == FN - 1)
        def _(b=b):
            b[N + HALO:N + 2 * HALO] = zero_halo

    for t in range(1, T):
        @pl.when(s == 0)
        def _(t=t):
            incs[t][...] = jnp.zeros(incs[t].shape, BF16)

    def halo(i, side):
        b = fields[i]
        if side == 0:
            src, dst, dev = b.at[HALO:2 * HALO], b.at[N + HALO:N + 2 * HALO], left
        else:
            src, dst, dev = b.at[N:N + HALO], b.at[0:HALO], right
        return pltpu.make_async_remote_copy(src_ref=src, dst_ref=dst, send_sem=hs.at[i, side], recv_sem=hr.at[i, side], device_id=dev, device_id_type=MESH)

    def send_halo(i, side):
        @pl.when(has_l if side == 0 else has_r)
        def _():
            halo(i, side).start()

    def wait_halo(i):
        @pl.when(has_r)
        def _():
            halo(i, 0).wait_recv()

        @pl.when(has_l)
        def _():
            halo(i, 1).wait_recv()

    def forward(t):
        return pltpu.make_async_remote_copy(src_ref=sent.at[t], dst_ref=incs[t + 1], send_sem=ssem.at[t], recv_sem=rsem.at[t], device_id=nxt, device_id_type=MESH)

    def step(b, right_b, r, cs):
        u = jnp.concatenate([b[r + HALO]] + [b[c] for c in cs], axis=1)
        w = jnp.concatenate([diag_v[r]] + [off_v[r, k] for k in range(K)], axis=1)
        corr = (right_b[r].astype(F32) - mm(u, w)).astype(BF16)
        return (b[r + HALO].astype(F32) + mm(corr, inv_v[r])).astype(BF16)

    order = [0, 1, N - 2, N - 1] + list(range(2, N - 2))
    stores = []
    for t in range(T):
        inc, rb, fa, fb = incs[t], rights[t], fields[2 * t], fields[2 * t + 1]
        if t == 0:
            for c in loads[:Q + 3]:
                c.wait()
        else:
            loads[Q + 4 + t].wait()

            @pl.when(has_p)
            def _(t=t):
                forward(t - 1).wait_recv()
        coupled = [mm(inc[q], coup_v[q]) for q in range(Q)]
        for n, r in enumerate(order):
            x = rhs_v[t, :, r * W:(r + 1) * W].astype(F32)
            for q in range(Q):
                x = x - jnp.where(e[q] == r, coupled[q], 0.0)
            x = x.astype(BF16)
            rb[r] = x
            fa[r + HALO] = mm(x, inv_v[r]).astype(BF16)
            if n == 3:
                if t == 0:
                    pl.semaphore_wait(barrier, has_l.astype(jnp.int32) + has_r.astype(jnp.int32) + has_p.astype(jnp.int32) + has_n.astype(jnp.int32))
                send_halo(2 * t, 0)
                send_halo(2 * t, 1)
        if t == 0:
            loads[Q + 3].wait()
            loads[Q + 4].wait()
        wait_halo(2 * t)
        for n, r in enumerate(order):
            fb[r + HALO] = step(fa, rb, r, local[r])
            if n == 3:
                send_halo(2 * t + 1, 0)
                send_halo(2 * t + 1, 1)
        wait_halo(2 * t + 1)
        if t + 1 < T:
            for q in range(Q):
                sent[t, q] = step(fb, rb, e[q], [col(e[q], k) for k in range(K)])

            @pl.when(has_n)
            def _(t=t):
                forward(t).start()
        for r in range(N):
            out_v[t, :, r * W:(r + 1) * W] = step(fb, rb, r, local[r])
        c = pltpu.make_async_copy(out_v.at[t], out.at[t, 0], st.at[t])
        c.start()
        stores.append(c)

    for i in range(2 * T):
        @pl.when(has_l)
        def _(i=i):
            halo(i, 0).wait_send()

        @pl.when(has_r)
        def _(i=i):
            halo(i, 1).wait_send()
    for t in range(T - 1):
        @pl.when(has_n)
        def _(t=t):
            forward(t).wait_send()
    for c in stores:
        c.wait()


def on_device(S, FN, rhs, inflow, diag, off, cols, inv, coup, iface):
    T, _, M, _ = rhs.shape
    _, N, K, W, _ = off.shape
    Q = coup.shape[1]
    ANY = pl.BlockSpec(memory_space=pl.ANY)
    SM = pl.BlockSpec(memory_space=pltpu.SMEM)
    DMA = pltpu.SemaphoreType.DMA
    return pl.pallas_call(
        functools.partial(kernel, S, FN, T, N, K, Q, W),
        out_shape=jax.ShapeDtypeStruct(rhs.shape, BF16),
        in_specs=[SM, SM] + [ANY] * 6,
        out_specs=ANY,
        scratch_shapes=[
            pltpu.VMEM((T, M, N * W), BF16),
            pltpu.VMEM((N, W, W), BF16),
            pltpu.VMEM((N, K, W, W), BF16),
            pltpu.VMEM((N, W, W), BF16),
            pltpu.VMEM((Q, W, W), BF16),
            pltpu.VMEM((T, M, N * W), BF16),
            pltpu.VMEM((T - 1, Q, M, W), BF16),
        ]
        + [pltpu.VMEM((Q, M, W), BF16)] * T
        + [pltpu.VMEM((N, M, W), BF16)] * T
        + [pltpu.VMEM((N + 2 * HALO, M, W), BF16)] * (2 * T)
        + [DMA((Q + 4 + T,)), DMA((T,)), DMA((2 * T, 2)), DMA((2 * T, 2)), DMA((T - 1,)), DMA((T - 1,))],
        compiler_params=pltpu.CompilerParams(collective_id=0, has_side_effects=True, vmem_limit_bytes=64000000),
        name="sweep",
    )(cols[0].T, iface, rhs, inflow, diag, off, inv, coup)


def solution(mesh):
    placed = (
        P(None, "slab", None, "face"),
        P("slab", None, "face"),
        P("slab", "face", None, None),
        P("slab", "face", None, None, None),
        P("slab", "face", None),
        P("slab", "face", None, None),
        P("slab", "face", None, None),
        P("face"),
    )
    return jax.shard_map(
        functools.partial(on_device, mesh.shape["slab"], mesh.shape["face"]),
        mesh=mesh,
        in_specs=placed,
        out_specs=P(None, "slab", None, "face"),
        check_vma=False,
    )
```

```python
import functools

import jax
import jax.numpy as jnp
from jax import lax
from jax.experimental import pallas as pl
from jax.experimental.pallas import tpu as pltpu
from jax.sharding import PartitionSpec as P

HALO = 2
MESH = pl.DeviceIdType.MESH
BF16 = jnp.bfloat16
F32 = jnp.float32


def mm(u, w):
    return lax.dot_general(u, w, (((1,), (1,)), ((), ())), preferred_element_type=F32)


def kernel(S, FN, T, N, K, Q, W, *refs):
    refs = list(refs)
    take = lambda n: [refs.pop(0) for _ in range(n)]
    cols, iface, rhs, inflow, diag, off, inv, coup = take(8)
    (out,) = take(1)
    rhs_v, diag_v, off_v, inv_v, coup_v, out_v, sent = take(7)
    z, part, ypart, h1send, y_in = take(5)
    incs = take(T)
    rights = take(T)
    f0, f1 = take(T), take(T)
    n0, o0, n1, o1 = take(T), take(T), take(T), take(T)
    ld, st, hs, hr, ysem, ssem, rsem = take(7)

    s = lax.axis_index("slab")
    f = lax.axis_index("face")
    odd = lax.rem(f, 2)
    has_o = (f > 0) & (f < FN - 1)
    has_p, has_n = s > 0, s < S - 1
    near = (s, f + 1 - 2 * odd)
    other = (s, jnp.clip(f - 1 + 2 * odd, 0, FN - 1))
    prev = (jnp.maximum(s - 1, 0), f)
    nxt = (jnp.minimum(s + 1, S - 1), f)
    oe = odd * (N - HALO)
    ne = (N - HALO) - oe
    o_slot = odd * (N + HALO)
    n_slot = (N + HALO) - o_slot

    barrier = pltpu.get_barrier_semaphore()
    pl.semaphore_signal(barrier, inc=1, device_id=near, device_id_type=MESH)
    for there, who in ((has_o, other), (has_p, prev), (has_n, nxt)):
        @pl.when(there)
        def _(who=who):
            pl.semaphore_signal(barrier, inc=1, device_id=who, device_id_type=MESH)

    loads = [pltpu.make_async_copy(inflow.at[0, :, q * W:(q + 1) * W], incs[0].at[q], ld.at[q]) for q in range(Q)]
    loads += [
        pltpu.make_async_copy(coup.at[0], coup_v, ld.at[Q]),
        pltpu.make_async_copy(rhs.at[0, 0], rhs_v.at[0], ld.at[Q + 1]),
        pltpu.make_async_copy(inv.at[0], inv_v, ld.at[Q + 2]),
        pltpu.make_async_copy(off.at[0], off_v, ld.at[Q + 4]),
        pltpu.make_async_copy(diag.at[0], diag_v, ld.at[Q + 3]),
    ]
    loads += [pltpu.make_async_copy(rhs.at[t, 0], rhs_v.at[t], ld.at[Q + 4 + t]) for t in range(1, T)]
    for c in loads:
        c.start()

    base = f * N - HALO

    def col(r, k):
        return jnp.clip(cols[k, r] - base, 0, N + 2 * HALO - 1)

    e = [iface[q] for q in range(Q)]

    zero_halo = jnp.zeros((HALO,) + f0[0].shape[1:], BF16)
    for b in f0 + f1:
        b[0:HALO] = zero_halo
        b[N + HALO:N + 2 * HALO] = zero_halo

    @pl.when(jnp.logical_not(has_o))
    def _():
        for b in o0 + o1:
            b[...] = zero_halo
        y_in[...] = jnp.zeros(y_in.shape, BF16)

    @pl.when(s == 0)
    def _():
        for b in incs[1:]:
            b[...] = jnp.zeros(b.shape, BF16)

    def to_near(i, src, dst):
        return pltpu.make_async_remote_copy(src_ref=src, dst_ref=dst, send_sem=hs.at[i, 0], recv_sem=hr.at[i, 0], device_id=near, device_id_type=MESH)

    def to_other(i, src, dst):
        return pltpu.make_async_remote_copy(src_ref=src, dst_ref=dst, send_sem=hs.at[i, 1], recv_sem=hr.at[i, 1], device_id=other, device_id_type=MESH)

    def copies(t):
        edge = lambda b, r: b.at[pl.ds(r + HALO, HALO)]
        return (
            to_near(2 * t, edge(f0[t], ne), n0[t]),
            to_other(2 * t, edge(f0[t], oe), o0[t]),
            to_near(2 * t + 1, edge(f1[t], ne), n1[t]),
            to_other(2 * t + 1, h1send.at[t], o1[t]),
        )

    def y_copy():
        return pltpu.make_async_remote_copy(src_ref=z.at[pl.ds(oe, HALO), :, HALO * W:2 * HALO * W], dst_ref=y_in, send_sem=ysem.at[0], recv_sem=ysem.at[1], device_id=other, device_id_type=MESH)

    def forward(t):
        return pltpu.make_async_remote_copy(src_ref=sent.at[t], dst_ref=incs[t + 1], send_sem=ssem.at[t], recv_sem=rsem.at[t], device_id=nxt, device_id_type=MESH)

    def when_o(act):
        @pl.when(has_o)
        def _():
            act()

    def own(b, right_b, r):
        u = jnp.concatenate([b[r + HALO]] + [b[col(r, k)] for k in range(K)], axis=1)
        w = jnp.concatenate([diag_v[r]] + [off_v[r, k] for k in range(K)], axis=1)
        corr = (right_b[r].astype(F32) - mm(u, w)).astype(BF16)
        return b[r + HALO].astype(F32) + mm(corr, inv_v[r])

    def halo_operator(r):
        tiles = [off_v[r, k].astype(F32) for k in range(K)]
        cs = [col(r, k) for k in range(K)]
        sums = []
        for slot in [n_slot + j for j in range(HALO)] + [o_slot + j for j in range(HALO)]:
            x = jnp.zeros((W, W), F32)
            for k in range(K):
                x = x + jnp.where(cs[k] == slot, tiles[k], 0.0)
            sums.append(x.astype(BF16))
        z[r] = jnp.dot(inv_v[r], jnp.concatenate(sums, axis=1), preferred_element_type=F32).astype(BF16)

    def pair(b):
        return jnp.concatenate([b[0], b[1]], axis=1)

    ZN, ZO = slice(0, HALO * W), slice(HALO * W, 2 * HALO * W)
    order = [oe, oe + 1, ne, ne + 1] + list(range(HALO, N - HALO))
    stores = []
    for t in range(T):
        inc, rb, fa, fb = incs[t], rights[t], f0[t], f1[t]
        near0, other0, near1, other1 = copies(t)
        if t == 0:
            for c in loads[:Q + 3]:
                c.wait()
        else:
            loads[Q + 4 + t].wait()

            @pl.when(has_p)
            def _(t=t):
                forward(t - 1).wait_recv()
        coupled = [mm(inc[q], coup_v[q]) for q in range(Q)]
        for n, r in enumerate(order):
            x = rhs_v[t, :, pl.ds(pl.multiple_of(r * W, W), W)].astype(F32)
            for q in range(Q):
                x = x - jnp.where(e[q] == r, coupled[q], 0.0)
            x = x.astype(BF16)
            rb[r] = x
            fa[r + HALO] = mm(x, inv_v[r]).astype(BF16)
            if n == 3:
                if t == 0:
                    pl.semaphore_wait(barrier, 1 + has_o.astype(jnp.int32) + has_p.astype(jnp.int32) + has_n.astype(jnp.int32))
                when_o(other0.start)
                near0.start()
        if t == 0:
            loads[Q + 3].wait()
            for r in order[:2]:
                halo_operator(r)
            when_o(lambda: y_copy().start())
            loads[Q + 4].wait()
        for r in order[:2]:
            part[r] = own(fa, rb, r)
        near0.wait_recv()
        hn = pair(n0[t])
        for i, r in enumerate(order[:2]):
            x = part[r] - mm(hn, z[r, :, ZN])
            part[r] = x
            h1send[t, i] = x.astype(BF16)
        when_o(other1.start)
        for r in order[2:]:
            if t == 0:
                halo_operator(r)
            part[r] = own(fa, rb, r) - mm(hn, z[r, :, ZN])
        if t == 0:
            when_o(lambda: y_copy().wait_recv())
        mine = jnp.concatenate([fa[oe + HALO], fa[oe + HALO + 1]], axis=1)
        for i in range(HALO):
            ypart[i] = mm(mine, y_in[i])
        when_o(other0.wait_recv)
        ho = pair(o0[t])
        for n, r in enumerate(order[2:4] + order[:2] + order[4:]):
            fb[r + HALO] = (part[r] - mm(ho, z[r, :, ZO])).astype(BF16)
            if n == 1:
                near1.start()
        if t + 1 < T:
            mid = [own(fb, rb, e[q]) for q in range(Q)]
        else:
            mid = []
            for r in range(N):
                part[r] = own(fb, rb, r)
        near1.wait_recv()
        when_o(other1.wait_recv)
        far = [(o1[t][i].astype(F32) - ypart[i]).astype(BF16) for i in range(HALO)]
        both = jnp.concatenate([n1[t][0], n1[t][1]] + far, axis=1)
        if t + 1 < T:
            for q in range(Q):
                sent[t, q] = (mid[q] - mm(both, z[e[q]])).astype(BF16)

            @pl.when(has_n)
            def _(t=t):
                forward(t).start()
            for r in range(N):
                part[r] = own(fb, rb, r)
        for r in range(N):
            out_v[t, :, r * W:(r + 1) * W] = (part[r] - mm(both, z[r])).astype(BF16)
        c = pltpu.make_async_copy(out_v.at[t], out.at[t, 0], st.at[t])
        c.start()
        stores.append(c)

    for t in range(T):
        near0, other0, near1, other1 = copies(t)
        near0.wait_send()
        near1.wait_send()
        when_o(other0.wait_send)
        when_o(other1.wait_send)
    when_o(lambda: y_copy().wait_send())
    for t in range(T - 1):
        @pl.when(has_n)
        def _(t=t):
            forward(t).wait_send()
    for c in stores:
        c.wait()


def on_device(S, FN, rhs, inflow, diag, off, cols, inv, coup, iface):
    T, _, M, _ = rhs.shape
    _, N, K, W, _ = off.shape
    Q = coup.shape[1]
    ANY = pl.BlockSpec(memory_space=pl.ANY)
    SM = pl.BlockSpec(memory_space=pltpu.SMEM)
    DMA = pltpu.SemaphoreType.DMA
    return pl.pallas_call(
        functools.partial(kernel, S, FN, T, N, K, Q, W),
        out_shape=jax.ShapeDtypeStruct(rhs.shape, BF16),
        in_specs=[SM, SM] + [ANY] * 6,
        out_specs=ANY,
        scratch_shapes=[
            pltpu.VMEM((T, M, N * W), BF16),
            pltpu.VMEM((N, W, W), BF16),
            pltpu.VMEM((N, K, W, W), BF16),
            pltpu.VMEM((N, W, W), BF16),
            pltpu.VMEM((Q, W, W), BF16),
            pltpu.VMEM((T, M, N * W), BF16),
            pltpu.VMEM((T - 1, Q, M, W), BF16),
        ]
        + [
            pltpu.VMEM((N, W, 2 * HALO * W), BF16),
            pltpu.VMEM((N, M, W), F32),
            pltpu.VMEM((HALO, M, W), F32),
            pltpu.VMEM((T, HALO, M, W), BF16),
            pltpu.VMEM((HALO, W, HALO * W), BF16),
        ]
        + [pltpu.VMEM((Q, M, W), BF16)] * T
        + [pltpu.VMEM((N, M, W), BF16)] * T
        + [pltpu.VMEM((N + 2 * HALO, M, W), BF16)] * (2 * T)
        + [pltpu.VMEM((HALO, M, W), BF16)] * (4 * T)
        + [DMA((Q + 4 + T,)), DMA((T,)), DMA((2 * T, 2)), DMA((2 * T, 2)), DMA((2,)), DMA((T - 1,)), DMA((T - 1,))],
        compiler_params=pltpu.CompilerParams(collective_id=0, has_side_effects=True, vmem_limit_bytes=64000000),
        name="sweep",
    )(cols[0].T, iface, rhs, inflow, diag, off, inv, coup)


def solution(mesh):
    placed = (
        P(None, "slab", None, "face"),
        P("slab", None, "face"),
        P("slab", "face", None, None),
        P("slab", "face", None, None, None),
        P("slab", "face", None),
        P("slab", "face", None, None),
        P("slab", "face", None, None),
        P("face"),
    )
    return jax.shard_map(
        functools.partial(on_device, mesh.shape["slab"], mesh.shape["face"]),
        mesh=mesh,
        in_specs=placed,
        out_specs=P(None, "slab", None, "face"),
        check_vma=False,
    )
```

```python
import functools

import jax
import jax.numpy as jnp
from jax import lax
from jax.experimental import pallas as pl
from jax.experimental.pallas import tpu as pltpu
from jax.sharding import PartitionSpec as P

HALO = 2
MESH = pl.DeviceIdType.MESH
BF16 = jnp.bfloat16
F32 = jnp.float32


def mm(u, w):
    return lax.dot_general(u, w, (((1,), (1,)), ((), ())), preferred_element_type=F32)


def kernel(S, FN, T, N, K, Q, W, *refs):
    refs = list(refs)
    take = lambda n: [refs.pop(0) for _ in range(n)]
    cols, iface, rhs, inflow, diag, off, inv, coup = take(8)
    (out,) = take(1)
    rhs_v, diag_v, off_v, inv_v, coup_v, out_v, sent = take(7)
    z, part, ypart, h1send, y_in = take(5)
    incs = take(T)
    rights = take(T)
    f0, f1 = take(T), take(T)
    n0, o0, n1, o1 = take(T), take(T), take(T), take(T)
    ld, st, hs, hr, ysem, ssem, rsem = take(7)

    s = lax.axis_index("slab")
    f = lax.axis_index("face")
    odd = lax.rem(f, 2)
    has_o = (f > 0) & (f < FN - 1)
    has_p, has_n = s > 0, s < S - 1
    near = (s, f + 1 - 2 * odd)
    other = (s, jnp.clip(f - 1 + 2 * odd, 0, FN - 1))
    prev = (jnp.maximum(s - 1, 0), f)
    nxt = (jnp.minimum(s + 1, S - 1), f)
    oe = odd * (N - HALO)
    ne = (N - HALO) - oe
    o_slot = odd * (N + HALO)
    n_slot = (N + HALO) - o_slot

    barrier = pltpu.get_barrier_semaphore()
    pl.semaphore_signal(barrier, inc=1, device_id=near, device_id_type=MESH)
    for there, who in ((has_o, other), (has_p, prev), (has_n, nxt)):
        @pl.when(there)
        def _(who=who):
            pl.semaphore_signal(barrier, inc=1, device_id=who, device_id_type=MESH)

    first = [
        pltpu.make_async_copy(inv.at[0], inv_v, ld.at[0]),
        pltpu.make_async_copy(rhs.at[0, 0], rhs_v.at[0], ld.at[1]),
        pltpu.make_async_copy(coup.at[0], coup_v, ld.at[2]),
    ]
    first += [pltpu.make_async_copy(inflow.at[0, :, q * W:(q + 1) * W], incs[0].at[q], ld.at[3 + q]) for q in range(Q)]
    tiles = [
        pltpu.make_async_copy(off.at[0], off_v, ld.at[3 + Q]),
        pltpu.make_async_copy(diag.at[0], diag_v, ld.at[4 + Q]),
    ]
    later = [pltpu.make_async_copy(rhs.at[t, 0], rhs_v.at[t], ld.at[4 + Q + t]) for t in range(1, T)]
    loads = first + tiles + later
    for c in loads:
        c.start()

    base = f * N - HALO

    def col(r, k):
        return jnp.clip(cols[k, r] - base, 0, N + 2 * HALO - 1)

    e = [iface[q] for q in range(Q)]

    zero_halo = jnp.zeros((HALO,) + f0[0].shape[1:], BF16)
    for b in f0 + f1:
        b[0:HALO] = zero_halo
        b[N + HALO:N + 2 * HALO] = zero_halo

    @pl.when(jnp.logical_not(has_o))
    def _():
        for b in o0 + o1:
            b[...] = zero_halo
        y_in[...] = jnp.zeros(y_in.shape, BF16)

    @pl.when(s == 0)
    def _():
        for b in incs[1:]:
            b[...] = jnp.zeros(b.shape, BF16)

    def to_near(i, src, dst):
        return pltpu.make_async_remote_copy(src_ref=src, dst_ref=dst, send_sem=hs.at[i, 0], recv_sem=hr.at[i, 0], device_id=near, device_id_type=MESH)

    def to_other(i, src, dst):
        return pltpu.make_async_remote_copy(src_ref=src, dst_ref=dst, send_sem=hs.at[i, 1], recv_sem=hr.at[i, 1], device_id=other, device_id_type=MESH)

    def copies(t):
        edge = lambda b, r: b.at[pl.ds(r + HALO, HALO)]
        return (
            to_near(2 * t, edge(f0[t], ne), n0[t]),
            to_other(2 * t, edge(f0[t], oe), o0[t]),
            to_near(2 * t + 1, edge(f1[t], ne), n1[t]),
            to_other(2 * t + 1, h1send.at[t], o1[t]),
        )

    def y_copy():
        return pltpu.make_async_remote_copy(src_ref=z.at[pl.ds(oe, HALO), :, HALO * W:2 * HALO * W], dst_ref=y_in, send_sem=ysem.at[0], recv_sem=ysem.at[1], device_id=other, device_id_type=MESH)

    def forward(t):
        return pltpu.make_async_remote_copy(src_ref=sent.at[t], dst_ref=incs[t + 1], send_sem=ssem.at[t], recv_sem=rsem.at[t], device_id=nxt, device_id_type=MESH)

    def when_o(act):
        @pl.when(has_o)
        def _():
            act()

    def own(b, right_b, r):
        u = jnp.concatenate([b[r + HALO]] + [b[col(r, k)] for k in range(K)], axis=1)
        w = jnp.concatenate([diag_v[r]] + [off_v[r, k] for k in range(K)], axis=1)
        corr = (right_b[r].astype(F32) - mm(u, w)).astype(BF16)
        return b[r + HALO].astype(F32) + mm(corr, inv_v[r])

    def halo_operator(r):
        tiles = [off_v[r, k].astype(F32) for k in range(K)]
        cs = [col(r, k) for k in range(K)]
        sums = []
        for slot in [n_slot + j for j in range(HALO)] + [o_slot + j for j in range(HALO)]:
            x = jnp.zeros((W, W), F32)
            for k in range(K):
                x = x + jnp.where(cs[k] == slot, tiles[k], 0.0)
            sums.append(x.astype(BF16))
        z[r] = jnp.dot(inv_v[r], jnp.concatenate(sums, axis=1), preferred_element_type=F32).astype(BF16)

    def pair(b):
        return jnp.concatenate([b[0], b[1]], axis=1)

    ZN, ZO = slice(0, HALO * W), slice(HALO * W, 2 * HALO * W)
    order = [oe, oe + 1, ne, ne + 1] + list(range(HALO, N - HALO))
    stores = []
    for t in range(T):
        inc, rb, fa, fb = incs[t], rights[t], f0[t], f1[t]
        near0, other0, near1, other1 = copies(t)
        if t == 0:
            for c in first:
                c.wait()
        else:
            later[t - 1].wait()

            @pl.when(has_p)
            def _(t=t):
                forward(t - 1).wait_recv()
        coupled = [mm(inc[q], coup_v[q]) for q in range(Q)]
        for n, r in enumerate(order):
            x = rhs_v[t, :, pl.ds(pl.multiple_of(r * W, W), W)].astype(F32)
            for q in range(Q):
                x = x - jnp.where(e[q] == r, coupled[q], 0.0)
            x = x.astype(BF16)
            rb[r] = x
            fa[r + HALO] = mm(x, inv_v[r]).astype(BF16)
            if n == 3 and t > 0:
                when_o(other0.start)
                near0.start()
        if t == 0:
            for c in tiles:
                c.wait()
            for r in order[:2]:
                halo_operator(r)
            pl.semaphore_wait(barrier, 1 + has_o.astype(jnp.int32) + has_p.astype(jnp.int32) + has_n.astype(jnp.int32))
            near0.start()
            when_o(other0.start)
            when_o(lambda: y_copy().start())
        for r in order[:2]:
            part[r] = own(fa, rb, r)
        near0.wait_recv()
        hn = pair(n0[t])
        for i, r in enumerate(order[:2]):
            x = part[r] - mm(hn, z[r, :, ZN])
            part[r] = x
            h1send[t, i] = x.astype(BF16)
        when_o(other1.start)
        for r in order[2:]:
            if t == 0:
                halo_operator(r)
            part[r] = own(fa, rb, r) - mm(hn, z[r, :, ZN])
        if t == 0:
            when_o(lambda: y_copy().wait_recv())
        mine = jnp.concatenate([fa[oe + HALO], fa[oe + HALO + 1]], axis=1)
        for i in range(HALO):
            ypart[i] = mm(mine, y_in[i])
        when_o(other0.wait_recv)
        ho = pair(o0[t])
        for n, r in enumerate(order[2:4] + order[:2] + order[4:]):
            fb[r + HALO] = (part[r] - mm(ho, z[r, :, ZO])).astype(BF16)
            if n == 1:
                near1.start()
        if t + 1 < T:
            mid = [own(fb, rb, e[q]) for q in range(Q)]
        else:
            mid = []
            for r in range(N):
                part[r] = own(fb, rb, r)
        near1.wait_recv()
        when_o(other1.wait_recv)
        far = [(o1[t][i].astype(F32) - ypart[i]).astype(BF16) for i in range(HALO)]
        both = jnp.concatenate([n1[t][0], n1[t][1]] + far, axis=1)
        if t + 1 < T:
            for q in range(Q):
                sent[t, q] = (mid[q] - mm(both, z[e[q]])).astype(BF16)

            @pl.when(has_n)
            def _(t=t):
                forward(t).start()
            for r in range(N):
                part[r] = own(fb, rb, r)
        for r in range(N):
            out_v[t, :, r * W:(r + 1) * W] = (part[r] - mm(both, z[r])).astype(BF16)
        c = pltpu.make_async_copy(out_v.at[t], out.at[t, 0], st.at[t])
        c.start()
        stores.append(c)

    for t in range(T):
        near0, other0, near1, other1 = copies(t)
        near0.wait_send()
        near1.wait_send()
        when_o(other0.wait_send)
        when_o(other1.wait_send)
    when_o(lambda: y_copy().wait_send())
    for t in range(T - 1):
        @pl.when(has_n)
        def _(t=t):
            forward(t).wait_send()
    for c in stores:
        c.wait()


def on_device(S, FN, rhs, inflow, diag, off, cols, inv, coup, iface):
    T, _, M, _ = rhs.shape
    _, N, K, W, _ = off.shape
    Q = coup.shape[1]
    ANY = pl.BlockSpec(memory_space=pl.ANY)
    SM = pl.BlockSpec(memory_space=pltpu.SMEM)
    DMA = pltpu.SemaphoreType.DMA
    return pl.pallas_call(
        functools.partial(kernel, S, FN, T, N, K, Q, W),
        out_shape=jax.ShapeDtypeStruct(rhs.shape, BF16),
        in_specs=[SM, SM] + [ANY] * 6,
        out_specs=ANY,
        scratch_shapes=[
            pltpu.VMEM((T, M, N * W), BF16),
            pltpu.VMEM((N, W, W), BF16),
            pltpu.VMEM((N, K, W, W), BF16),
            pltpu.VMEM((N, W, W), BF16),
            pltpu.VMEM((Q, W, W), BF16),
            pltpu.VMEM((T, M, N * W), BF16),
            pltpu.VMEM((T - 1, Q, M, W), BF16),
        ]
        + [
            pltpu.VMEM((N, W, 2 * HALO * W), BF16),
            pltpu.VMEM((N, M, W), F32),
            pltpu.VMEM((HALO, M, W), F32),
            pltpu.VMEM((T, HALO, M, W), BF16),
            pltpu.VMEM((HALO, W, HALO * W), BF16),
        ]
        + [pltpu.VMEM((Q, M, W), BF16)] * T
        + [pltpu.VMEM((N, M, W), BF16)] * T
        + [pltpu.VMEM((N + 2 * HALO, M, W), BF16)] * (2 * T)
        + [pltpu.VMEM((HALO, M, W), BF16)] * (4 * T)
        + [DMA((4 + Q + T,)), DMA((T,)), DMA((2 * T, 2)), DMA((2 * T, 2)), DMA((2,)), DMA((T - 1,)), DMA((T - 1,))],
        compiler_params=pltpu.CompilerParams(collective_id=0, has_side_effects=True, vmem_limit_bytes=48000000),
        name="sweep",
    )(*[pltpu.with_memory_space_constraint(x, pltpu.HBM) for x in (cols[0].T, iface, rhs, inflow, diag, off, inv, coup)])


def solution(mesh):
    placed = (
        P(None, "slab", None, "face"),
        P("slab", None, "face"),
        P("slab", "face", None, None),
        P("slab", "face", None, None, None),
        P("slab", "face", None),
        P("slab", "face", None, None),
        P("slab", "face", None, None),
        P("face"),
    )
    return jax.shard_map(
        functools.partial(on_device, mesh.shape["slab"], mesh.shape["face"]),
        mesh=mesh,
        in_specs=placed,
        out_specs=P(None, "slab", None, "face"),
        check_vma=False,
    )
```

```python
import functools

import jax
import jax.numpy as jnp
from jax import lax
from jax.experimental import pallas as pl
from jax.experimental.pallas import tpu as pltpu
from jax.sharding import PartitionSpec as P

HALO = 2
DIAGONAL_FROM = 1
MESH = pl.DeviceIdType.MESH
BF16 = jnp.bfloat16
F32 = jnp.float32


def mm(u, w):
    return lax.dot_general(u, w, (((1,), (1,)), ((), ())), preferred_element_type=F32)


def kernel(S, FN, T, N, K, Q, W, *refs):
    refs = list(refs)
    take = lambda n: [refs.pop(0) for _ in range(n)]
    cols, iface, rhs, inflow, diag, off, inv, coup = take(8)
    (out,) = take(1)
    rhs_v, diag_v, off_v, inv_v, coup_v, out_v, sent = take(7)
    z, part, ypart, h1send, y_in = take(5)
    fp, p_send, p_near, p_near_in, d_near, d_near_in, e0, e0_in, e1, e1_in, dinc = take(11)
    incs = take(T)
    rights = take(T)
    f0, f1 = take(T), take(T)
    n0, o0, n1, o1 = take(T), take(T), take(T), take(T)
    ld, st, hs, hr, ysem, ssem, rsem, es, ps, ds, dr = take(11)

    s = lax.axis_index("slab")
    f = lax.axis_index("face")
    odd = lax.rem(f, 2)
    has_o = (f > 0) & (f < FN - 1)
    has_p, has_n = s > 0, s < S - 1
    near = (s, f + 1 - 2 * odd)
    other = (s, jnp.clip(f - 1 + 2 * odd, 0, FN - 1))
    prev = (jnp.maximum(s - 1, 0), f)
    nxt = (jnp.minimum(s + 1, S - 1), f)
    SE = FN // 2
    seam = (f == SE - 1) | (f == SE)
    duo = (f >= SE - 2) & (f <= SE + 1)
    mate = duo & jnp.logical_not(seam)
    plain_o = has_o & jnp.logical_not(seam)
    across = jnp.where(f < SE, SE, SE - 1)
    slot = jnp.where(seam, 0, 1)
    oe = odd * (N - HALO)
    ne = (N - HALO) - oe
    o_slot = odd * (N + HALO)
    n_slot = (N + HALO) - o_slot

    barrier = pltpu.get_barrier_semaphore()
    pl.semaphore_signal(barrier, inc=1, device_id=near, device_id_type=MESH)
    greeted = ((has_o, other), (has_p, prev), (has_n, nxt), (duo & has_n, (nxt[0], across)), (seam & has_p, (prev[0], across)), (seam & has_p, (prev[0], jnp.where(f < SE, SE + 1, SE - 2))))
    for there, who in greeted:
        @pl.when(there)
        def _(who=who):
            pl.semaphore_signal(barrier, inc=1, device_id=who, device_id_type=MESH)

    first = [
        pltpu.make_async_copy(inv.at[0], inv_v, ld.at[0]),
        pltpu.make_async_copy(rhs.at[0, 0], rhs_v.at[0], ld.at[1]),
        pltpu.make_async_copy(coup.at[0], coup_v, ld.at[2]),
    ]
    first += [pltpu.make_async_copy(inflow.at[0, :, q * W:(q + 1) * W], incs[0].at[q], ld.at[3 + q]) for q in range(Q)]
    tiles = [
        pltpu.make_async_copy(off.at[0], off_v, ld.at[3 + Q]),
        pltpu.make_async_copy(diag.at[0], diag_v, ld.at[4 + Q]),
    ]
    later = [pltpu.make_async_copy(rhs.at[t, 0], rhs_v.at[t], ld.at[4 + Q + t]) for t in range(1, T)]
    loads = first + tiles + later
    for c in loads:
        c.start()

    base = f * N - HALO

    def col(r, k):
        return jnp.clip(cols[k, r] - base, 0, N + 2 * HALO - 1)

    e = [iface[q] for q in range(Q)]

    zero_halo = jnp.zeros((HALO,) + f0[0].shape[1:], BF16)
    for b in f0 + f1 + [fp]:
        b[0:HALO] = zero_halo
        b[N + HALO:N + 2 * HALO] = zero_halo

    @pl.when(jnp.logical_not(has_o))
    def _():
        for b in o0 + o1:
            b[...] = zero_halo
        y_in[...] = jnp.zeros(y_in.shape, BF16)

    @pl.when(s == 0)
    def _():
        for b in incs[1:]:
            b[...] = jnp.zeros(b.shape, BF16)

    @pl.when((s == 0) & seam)
    def _():
        dinc[...] = jnp.zeros(dinc.shape, BF16)

    def to_near(i, src, dst):
        return pltpu.make_async_remote_copy(src_ref=src, dst_ref=dst, send_sem=hs.at[i, 0], recv_sem=hr.at[i, 0], device_id=near, device_id_type=MESH)

    def to_other(i, src, dst):
        return pltpu.make_async_remote_copy(src_ref=src, dst_ref=dst, send_sem=hs.at[i, 1], recv_sem=hr.at[i, 1], device_id=other, device_id_type=MESH)

    def copies(t):
        edge = lambda b, r: b.at[pl.ds(r + HALO, HALO)]
        return (
            to_near(2 * t, edge(f0[t], ne), n0[t]),
            to_other(2 * t, edge(f0[t], oe), o0[t]),
            to_near(2 * t + 1, edge(f1[t], ne), n1[t]),
            to_other(2 * t + 1, h1send.at[t], o1[t]),
        )

    def y_copy():
        return pltpu.make_async_remote_copy(src_ref=z.at[pl.ds(oe, HALO), :, HALO * W:2 * HALO * W], dst_ref=y_in, send_sem=ysem.at[0], recv_sem=ysem.at[1], device_id=other, device_id_type=MESH)

    def forward(t):
        return pltpu.make_async_remote_copy(src_ref=sent.at[t], dst_ref=incs[t + 1], send_sem=ssem.at[t], recv_sem=rsem.at[t], device_id=nxt, device_id_type=MESH)

    def diagonal(t, i):
        return pltpu.make_async_remote_copy(src_ref=sent.at[t], dst_ref=dinc.at[t, i], send_sem=ds.at[t], recv_sem=dr.at[t, i], device_id=(nxt[0], across), device_id_type=MESH)

    def swap(src, dst, sems, i, dev):
        return pltpu.make_async_remote_copy(src_ref=src, dst_ref=dst, send_sem=sems.at[2 * i], recv_sem=sems.at[2 * i + 1], device_id=dev, device_id_type=MESH)

    e_copies = [swap(e0, e0_in, es, 0, other), swap(e1, e1_in, es, 1, other)]
    mate_copies = [swap(d_near, d_near_in, ps, 0, near), swap(p_near, p_near_in, ps, 1, near)]

    def when_o(act):
        @pl.when(has_o)
        def _():
            act()

    def own(b, right_r, r):
        u = jnp.concatenate([b[r + HALO]] + [b[col(r, k)] for k in range(K)], axis=1)
        w = jnp.concatenate([diag_v[r]] + [off_v[r, k] for k in range(K)], axis=1)
        corr = (right_r.astype(F32) - mm(u, w)).astype(BF16)
        return b[r + HALO].astype(F32) + mm(corr, inv_v[r])

    def halo_operator(r):
        tiles = [off_v[r, k].astype(F32) for k in range(K)]
        cs = [col(r, k) for k in range(K)]
        sums = []
        for slot in [n_slot + j for j in range(HALO)] + [o_slot + j for j in range(HALO)]:
            x = jnp.zeros((W, W), F32)
            for k in range(K):
                x = x + jnp.where(cs[k] == slot, tiles[k], 0.0)
            sums.append(x.astype(BF16))
        z[r] = jnp.dot(inv_v[r], jnp.concatenate(sums, axis=1), preferred_element_type=F32).astype(BF16)

    def pair(b):
        return jnp.concatenate([b[0], b[1]], axis=1)

    ZN, ZO = slice(0, HALO * W), slice(HALO * W, 2 * HALO * W)

    def nn(a, b):
        return jnp.dot(a, b, preferred_element_type=F32)

    def rhs_row(t, r):
        return rhs_v[t, :, pl.ds(pl.multiple_of(r * W, W), W)]

    d = []

    def placed(r):
        return jnp.concatenate([jnp.where(e[q] == r, d[q].astype(F32), 0.0) for q in range(Q)], axis=1)

    def mate_setup():
        d.extend(nn(inv_v[e[q]], coup_v[q]).astype(BF16) for q in range(Q))

        @pl.when(mate)
        def _():
            for j in range(HALO):
                d_near[j] = placed(ne + j).astype(BF16)
            mate_copies[0].start()
            for t in range(1, T):
                later[t - 1].wait()
                for j in range(HALO):
                    p_near[t - 1, j] = mm(rhs_row(t, ne + j), inv_v[ne + j]).astype(BF16)
            mate_copies[1].start()

        @pl.when(jnp.logical_not(mate))
        def _():
            for c in later:
                c.wait()

    def seam_operators():
        @pl.when(seam)
        def _():
            mate_copies[0].wait_recv()
            below = jnp.concatenate([d_near_in[j] for j in range(HALO)], axis=0)
            for i in range(HALO):
                r = oe + i
                cs = [col(r, k) for k in range(K)]
                at = []
                for q in range(Q):
                    x = jnp.where(e[q] == r, diag_v[r].astype(F32), 0.0)
                    for k in range(K):
                        x = x + jnp.where(cs[k] == e[q] + HALO, off_v[r, k].astype(F32), 0.0)
                    at.append(x.astype(BF16))
                y = nn(inv_v[r], jnp.concatenate(at, axis=1)).astype(BF16)
                d_r = placed(r)
                e0[i] = d_r.astype(BF16)
                mine = jnp.concatenate([nn(y[:, q * W:(q + 1) * W], d[q]) for q in range(Q)], axis=1)
                e1[i, :, 0:Q * W] = (2.0 * d_r - mine).astype(BF16)
                e1[i, :, Q * W:2 * Q * W] = (-nn(z[r, :, ZN], below)).astype(BF16)
            for c in e_copies:
                c.start()

    def seam_rows(t):
        @pl.when(seam)
        def _():
            if t == DIAGONAL_FROM:
                mate_copies[1].wait_recv()
            for r in range(N):
                fp[r + HALO] = mm(rhs_row(t, r), inv_v[r]).astype(BF16)
            hn = jnp.concatenate([p_near_in[t - 1, j] for j in range(HALO)], axis=1)
            for i in range(HALO):
                p_send[t - 1, 0, i] = fp[oe + HALO + i]
                p_send[t - 1, 1, i] = (own(fp, rhs_row(t, oe + i), oe + i) - mm(hn, z[oe + i, :, ZN])).astype(BF16)
            to_other(2 * t, p_send.at[t - 1, 0], o0[t]).start()
            to_other(2 * t + 1, p_send.at[t - 1, 1], o1[t]).start()

    def complete(t, b, op, n):
        vals = jnp.concatenate([dinc[t - 1, i, q] for i in range(n) for q in range(Q)], axis=1)
        for j in range(HALO):
            b[j] = (b[j].astype(F32) - mm(vals, op[j])).astype(BF16)
    order = [oe, oe + 1, ne, ne + 1] + list(range(HALO, N - HALO))
    stores = []
    for t in range(T):
        inc, rb, fa, fb = incs[t], rights[t], f0[t], f1[t]
        near0, other0, near1, other1 = copies(t)
        crossing = has_o if t < DIAGONAL_FROM else plain_o
        if t == 0:
            for c in first:
                c.wait()
        else:
            @pl.when(has_p)
            def _(t=t):
                forward(t - 1).wait_recv()
        coupled = [mm(inc[q], coup_v[q]) for q in range(Q)]
        for n, r in enumerate(order):
            x = rhs_row(t, r).astype(F32)
            for q in range(Q):
                x = x - jnp.where(e[q] == r, coupled[q], 0.0)
            x = x.astype(BF16)
            rb[r] = x
            fa[r + HALO] = mm(x, inv_v[r]).astype(BF16)
            if n == 3 and t > 0:
                pl.when(crossing)(other0.start)
                near0.start()
        if t == 0:
            for c in tiles:
                c.wait()
            for r in order[:2]:
                halo_operator(r)
            pl.semaphore_wait(barrier, 1 + sum(there.astype(jnp.int32) for there, _ in greeted))
            near0.start()
            when_o(other0.start)
            when_o(lambda: y_copy().start())
        for r in order[:2]:
            part[r] = own(fa, rb[r], r)
        near0.wait_recv()
        hn = pair(n0[t])
        for i, r in enumerate(order[:2]):
            x = part[r] - mm(hn, z[r, :, ZN])
            part[r] = x
            h1send[t, i] = x.astype(BF16)
        pl.when(crossing)(other1.start)
        if t == 0:
            mate_setup()
        if DIAGONAL_FROM <= t + 1 < T:
            seam_rows(t + 1)
        if t == 0:
            seam_operators()
        for r in order[2:]:
            if t == 0:
                halo_operator(r)
            part[r] = own(fa, rb[r], r) - mm(hn, z[r, :, ZN])
        if t == 0:
            when_o(lambda: y_copy().wait_recv())
        mine = jnp.concatenate([fa[oe + HALO], fa[oe + HALO + 1]], axis=1)
        for i in range(HALO):
            ypart[i] = mm(mine, y_in[i])
        when_o(other0.wait_recv)
        if t >= DIAGONAL_FROM:
            @pl.when(seam)
            def _(t=t):
                if t == DIAGONAL_FROM:
                    for c in e_copies:
                        c.wait_recv()

                @pl.when(has_p)
                def _():
                    for i in range(2):
                        diagonal(t - 1, i).wait_recv()
                complete(t, o0[t], e0_in, 1)
        ho = pair(o0[t])
        for n, r in enumerate(order[2:4] + order[:2] + order[4:]):
            fb[r + HALO] = (part[r] - mm(ho, z[r, :, ZO])).astype(BF16)
            if n == 1:
                near1.start()
        if t + 1 < T:
            mid = [own(fb, rb[e[q]], e[q]) for q in range(Q)]
        else:
            mid = []
            for r in range(N):
                part[r] = own(fb, rb[r], r)
        when_o(other1.wait_recv)
        if t >= DIAGONAL_FROM:
            @pl.when(seam)
            def _(t=t):
                complete(t, o1[t], e1_in, 2)
        near1.wait_recv()
        far = [(o1[t][i].astype(F32) - ypart[i]).astype(BF16) for i in range(HALO)]
        both = jnp.concatenate([n1[t][0], n1[t][1]] + far, axis=1)
        if t + 1 < T:
            for q in range(Q):
                sent[t, q] = (mid[q] - mm(both, z[e[q]])).astype(BF16)

            @pl.when(has_n)
            def _(t=t):
                forward(t).start()

            if t + 1 >= DIAGONAL_FROM:
                @pl.when(has_n & duo)
                def _(t=t):
                    diagonal(t, slot).start()
            for r in range(N):
                part[r] = own(fb, rb[r], r)
        for r in range(N):
            out_v[t, :, r * W:(r + 1) * W] = (part[r] - mm(both, z[r])).astype(BF16)
        c = pltpu.make_async_copy(out_v.at[t], out.at[t, 0], st.at[t])
        c.start()
        stores.append(c)

    for t in range(T):
        near0, other0, near1, other1 = copies(t)
        near0.wait_send()
        near1.wait_send()
        when_o(other0.wait_send)
        when_o(other1.wait_send)
    when_o(lambda: y_copy().wait_send())
    for t in range(T - 1):
        @pl.when(has_n)
        def _(t=t):
            forward(t).wait_send()

        if t + 1 >= DIAGONAL_FROM:
            @pl.when(has_n & duo)
            def _(t=t):
                diagonal(t, slot).wait_send()

    @pl.when(seam)
    def _():
        for c in e_copies:
            c.wait_send()

    @pl.when(mate)
    def _():
        for c in mate_copies:
            c.wait_send()
    for c in stores:
        c.wait()


def on_device(S, FN, rhs, inflow, diag, off, cols, inv, coup, iface):
    T, _, M, _ = rhs.shape
    _, N, K, W, _ = off.shape
    Q = coup.shape[1]
    ANY = pl.BlockSpec(memory_space=pl.ANY)
    SM = pl.BlockSpec(memory_space=pltpu.SMEM)
    DMA = pltpu.SemaphoreType.DMA
    return pl.pallas_call(
        functools.partial(kernel, S, FN, T, N, K, Q, W),
        out_shape=jax.ShapeDtypeStruct(rhs.shape, BF16),
        in_specs=[SM, SM] + [ANY] * 6,
        out_specs=ANY,
        scratch_shapes=[
            pltpu.VMEM((T, M, N * W), BF16),
            pltpu.VMEM((N, W, W), BF16),
            pltpu.VMEM((N, K, W, W), BF16),
            pltpu.VMEM((N, W, W), BF16),
            pltpu.VMEM((Q, W, W), BF16),
            pltpu.VMEM((T, M, N * W), BF16),
            pltpu.VMEM((T - 1, Q, M, W), BF16),
        ]
        + [
            pltpu.VMEM((N, W, 2 * HALO * W), BF16),
            pltpu.VMEM((N, M, W), F32),
            pltpu.VMEM((HALO, M, W), F32),
            pltpu.VMEM((T, HALO, M, W), BF16),
            pltpu.VMEM((HALO, W, HALO * W), BF16),
            pltpu.VMEM((N + 2 * HALO, M, W), BF16),
            pltpu.VMEM((T - 1, 2, HALO, M, W), BF16),
            pltpu.VMEM((T - 1, HALO, M, W), BF16),
            pltpu.VMEM((T - 1, HALO, M, W), BF16),
            pltpu.VMEM((HALO, W, Q * W), BF16),
            pltpu.VMEM((HALO, W, Q * W), BF16),
            pltpu.VMEM((HALO, W, Q * W), BF16),
            pltpu.VMEM((HALO, W, Q * W), BF16),
            pltpu.VMEM((HALO, W, 2 * Q * W), BF16),
            pltpu.VMEM((HALO, W, 2 * Q * W), BF16),
            pltpu.VMEM((T - 1, 2, Q, M, W), BF16),
        ]
        + [pltpu.VMEM((Q, M, W), BF16)] * T
        + [pltpu.VMEM((N, M, W), BF16)] * T
        + [pltpu.VMEM((N + 2 * HALO, M, W), BF16)] * (2 * T)
        + [pltpu.VMEM((HALO, M, W), BF16)] * (4 * T)
        + [DMA((4 + Q + T,)), DMA((T,)), DMA((2 * T, 2)), DMA((2 * T, 2)), DMA((2,)), DMA((T - 1,)), DMA((T - 1,)), DMA((4,)), DMA((4,)), DMA((T - 1,)), DMA((T - 1, 2))],
        compiler_params=pltpu.CompilerParams(collective_id=0, has_side_effects=True, vmem_limit_bytes=48000000),
        name="sweep",
    )(*[pltpu.with_memory_space_constraint(x, pltpu.HBM) for x in (cols[0].T, iface, rhs, inflow, diag, off, inv, coup)])


def solution(mesh):
    placed = (
        P(None, "slab", None, "face"),
        P("slab", None, "face"),
        P("slab", "face", None, None),
        P("slab", "face", None, None, None),
        P("slab", "face", None),
        P("slab", "face", None, None),
        P("slab", "face", None, None),
        P("face"),
    )
    return jax.shard_map(
        functools.partial(on_device, mesh.shape["slab"], mesh.shape["face"]),
        mesh=mesh,
        in_specs=placed,
        out_specs=P(None, "slab", None, "face"),
        check_vma=False,
    )
```

```python
import functools

import jax
import jax.numpy as jnp
from jax import lax
from jax.experimental import pallas as pl
from jax.experimental.pallas import tpu as pltpu
from jax.sharding import PartitionSpec as P

HALO = 2
DIAGONAL_FROM = 1
MESH = pl.DeviceIdType.MESH
BF16 = jnp.bfloat16
F32 = jnp.float32


def mm(u, w):
    return lax.dot_general(u, w, (((1,), (1,)), ((), ())), preferred_element_type=F32)


def kernel(S, FN, T, N, K, Q, W, *refs):
    refs = list(refs)
    take = lambda n: [refs.pop(0) for _ in range(n)]
    cols, iface, rhs, inflow, diag, off, inv, coup = take(8)
    (out,) = take(1)
    rhs_v, diag_v, off_v, inv_v, coup_v, out_v, sent = take(7)
    z, part, ypart, h1send, y_in, g = take(6)
    fp, p_send, p_near, p_near_in, d_near, d_near_in, e0, e0_in, e1, e1_in, dinc = take(11)
    incs = take(T)
    f0, f1 = take(T), take(T)
    n0, o0, n1, o1 = take(T), take(T), take(T), take(T)
    ld, st, hs, hr, ysem, ssem, rsem, es, ps, ds, dr = take(11)

    s = lax.axis_index("slab")
    f = lax.axis_index("face")
    odd = lax.rem(f, 2)
    has_o = (f > 0) & (f < FN - 1)
    has_p, has_n = s > 0, s < S - 1
    near = (s, f + 1 - 2 * odd)
    other = (s, jnp.clip(f - 1 + 2 * odd, 0, FN - 1))
    prev = (jnp.maximum(s - 1, 0), f)
    nxt = (jnp.minimum(s + 1, S - 1), f)
    SE = FN // 2
    seam = (f == SE - 1) | (f == SE)
    duo = (f >= SE - 2) & (f <= SE + 1)
    mate = duo & jnp.logical_not(seam)
    plain_o = has_o & jnp.logical_not(seam)
    across = jnp.where(f < SE, SE, SE - 1)
    slot = jnp.where(seam, 0, 1)
    oe = odd * (N - HALO)
    ne = (N - HALO) - oe
    o_slot = odd * (N + HALO)
    n_slot = (N + HALO) - o_slot

    barrier = pltpu.get_barrier_semaphore()
    pl.semaphore_signal(barrier, inc=1, device_id=near, device_id_type=MESH)
    greeted = ((has_o, other), (has_p, prev), (has_n, nxt), (duo & has_n, (nxt[0], across)), (seam & has_p, (prev[0], across)), (seam & has_p, (prev[0], jnp.where(f < SE, SE + 1, SE - 2))))
    for there, who in greeted:
        @pl.when(there)
        def _(who=who):
            pl.semaphore_signal(barrier, inc=1, device_id=who, device_id_type=MESH)

    first = [
        pltpu.make_async_copy(inv.at[0], inv_v, ld.at[0]),
        pltpu.make_async_copy(rhs.at[0, 0], rhs_v.at[0], ld.at[1]),
        pltpu.make_async_copy(coup.at[0], coup_v, ld.at[2]),
    ]
    first += [pltpu.make_async_copy(inflow.at[0, :, q * W:(q + 1) * W], incs[0].at[q], ld.at[3 + q]) for q in range(Q)]
    tiles = [
        pltpu.make_async_copy(off.at[0], off_v, ld.at[3 + Q]),
        pltpu.make_async_copy(diag.at[0], diag_v, ld.at[4 + Q]),
    ]
    later = [pltpu.make_async_copy(rhs.at[t, 0], rhs_v.at[t], ld.at[4 + Q + t]) for t in range(1, T)]
    loads = first + tiles + later
    for c in loads:
        c.start()

    base = f * N - HALO

    def col(r, k):
        return jnp.clip(cols[k, r] - base, 0, N + 2 * HALO - 1)

    zero_halo = jnp.zeros((HALO,) + f0[0].shape[1:], BF16)
    for b in f0 + f1 + [fp]:
        b[0:HALO] = zero_halo
        b[N + HALO:N + 2 * HALO] = zero_halo

    @pl.when(jnp.logical_not(has_o))
    def _():
        for b in o0 + o1:
            b[...] = zero_halo
        y_in[...] = jnp.zeros(y_in.shape, BF16)

    @pl.when(s == 0)
    def _():
        for b in incs[1:]:
            b[...] = jnp.zeros(b.shape, BF16)

    @pl.when((s == 0) & seam)
    def _():
        dinc[...] = jnp.zeros(dinc.shape, BF16)

    e = [iface[q] for q in range(Q)]

    def to_near(i, src, dst):
        return pltpu.make_async_remote_copy(src_ref=src, dst_ref=dst, send_sem=hs.at[i, 0], recv_sem=hr.at[i, 0], device_id=near, device_id_type=MESH)

    def to_other(i, src, dst):
        return pltpu.make_async_remote_copy(src_ref=src, dst_ref=dst, send_sem=hs.at[i, 1], recv_sem=hr.at[i, 1], device_id=other, device_id_type=MESH)

    def copies(t):
        edge = lambda b, r: b.at[pl.ds(r + HALO, HALO)]
        return (
            to_near(2 * t, edge(f0[t], ne), n0[t]),
            to_other(2 * t, edge(f0[t], oe), o0[t]),
            to_near(2 * t + 1, edge(f1[t], ne), n1[t]),
            to_other(2 * t + 1, h1send.at[t], o1[t]),
        )

    def y_copy():
        return pltpu.make_async_remote_copy(src_ref=z.at[pl.ds(oe, HALO), :, (N + HALO) * W:(N + 2 * HALO) * W], dst_ref=y_in, send_sem=ysem.at[0], recv_sem=ysem.at[1], device_id=other, device_id_type=MESH)

    def forward(t):
        return pltpu.make_async_remote_copy(src_ref=sent.at[t], dst_ref=incs[t + 1], send_sem=ssem.at[t], recv_sem=rsem.at[t], device_id=nxt, device_id_type=MESH)

    def diagonal(t, i):
        return pltpu.make_async_remote_copy(src_ref=sent.at[t], dst_ref=dinc.at[t, i], send_sem=ds.at[t], recv_sem=dr.at[t, i], device_id=(nxt[0], across), device_id_type=MESH)

    def swap(src, dst, sems, i, dev):
        return pltpu.make_async_remote_copy(src_ref=src, dst_ref=dst, send_sem=sems.at[2 * i], recv_sem=sems.at[2 * i + 1], device_id=dev, device_id_type=MESH)

    e_copies = [swap(e0, e0_in, es, 0, other), swap(e1, e1_in, es, 1, other)]
    mate_copies = [swap(d_near, d_near_in, ps, 0, near), swap(p_near, p_near_in, ps, 1, near)]

    def when_o(act):
        @pl.when(has_o)
        def _():
            act()

    def operator_rows(r):
        prod = jnp.dot(inv_v[r], jnp.concatenate([diag_v[r]] + [off_v[r, k] for k in range(K)], axis=1), preferred_element_type=F32)
        prod = prod.astype(BF16)
        tiles = [prod[:, k * W:(k + 1) * W] for k in range(K + 1)]
        cs = [r + HALO] + [col(r, k) for k in range(K)]
        slots = [c + HALO for c in range(N)] + [n_slot + j for j in range(HALO)] + [o_slot + j for j in range(HALO)]
        for c, slot in enumerate(slots):
            x = None
            for k in range(0 if c < N else 1, K + 1):
                y = jnp.where(cs[k] == slot, tiles[k], jnp.zeros((), BF16))
                x = y if x is None else x + y
            z[r, :, c * W:(c + 1) * W] = x

    def block_of(b):
        return jnp.concatenate([b[c + HALO] for c in range(N)], axis=1)

    OWN, ZN, ZO = slice(0, N * W), slice(N * W, (N + HALO) * W), slice((N + HALO) * W, (N + 2 * HALO) * W)
    HALOS = slice(N * W, (N + 2 * HALO) * W)

    def own(b, p):
        return [b[p + i + HALO].astype(F32) + g[p + i] - x for i, x in enumerate(halo_term(block_of(b), p, OWN))]

    def rows_of(p, q, part_of):
        return jnp.concatenate([z[p, :, part_of], z[q, :, part_of]], axis=0)

    def halo_term(v, p, part_of):
        x = mm(v, z[pl.ds(p, 2), :, part_of].reshape(2 * W, v.shape[1]))
        return x[:, :W], x[:, W:]

    def pair(b):
        return jnp.concatenate([b[0], b[1]], axis=1)


    def nn(a, b):
        return jnp.dot(a, b, preferred_element_type=F32)

    order = [oe, oe + 1, ne, ne + 1] + list(range(HALO, N - HALO))

    def rhs_row(t, r):
        return rhs_v[t, :, pl.ds(pl.multiple_of(r * W, W), W)]

    d = []

    def placed(r):
        return jnp.concatenate([jnp.where(e[q] == r, d[q].astype(F32), 0.0) for q in range(Q)], axis=1)

    def mate_setup():
        d.extend(nn(inv_v[e[q]], coup_v[q]).astype(BF16) for q in range(Q))

        @pl.when(mate)
        def _():
            for j in range(HALO):
                d_near[j] = placed(ne + j).astype(BF16)
            mate_copies[0].start()
            for t in range(1, T):
                later[t - 1].wait()
                for j in range(HALO):
                    p_near[t - 1, j] = mm(rhs_row(t, ne + j), inv_v[ne + j]).astype(BF16)
            mate_copies[1].start()

        @pl.when(jnp.logical_not(mate))
        def _():
            for c in later:
                c.wait()

    def own_tile(r, c):
        x = jnp.zeros((W, W), BF16)
        for j in range(N):
            x = x + jnp.where(c == j, z[r, :, j * W:(j + 1) * W], jnp.zeros((), BF16))
        return x

    def seam_operators():
        @pl.when(seam)
        def _():
            mate_copies[0].wait_recv()
            below = jnp.concatenate([d_near_in[j] for j in range(HALO)], axis=0)
            for i in range(HALO):
                r = oe + i
                d_r = placed(r)
                e0[i] = d_r.astype(BF16)
                mine = jnp.concatenate([nn(own_tile(r, e[q]), d[q]) for q in range(Q)], axis=1)
                e1[i, :, 0:Q * W] = (2.0 * d_r - mine).astype(BF16)
                e1[i, :, Q * W:2 * Q * W] = (-nn(z[r, :, ZN], below)).astype(BF16)
            for c in e_copies:
                c.start()

    def seam_rows(t):
        @pl.when(seam)
        def _():
            if t == DIAGONAL_FROM:
                mate_copies[1].wait_recv()
            edge = []
            for r in order:
                x = mm(rhs_row(t, r), inv_v[r])
                fp[r + HALO] = x.astype(BF16)
                if len(edge) < HALO:
                    edge.append(x)
            hn = jnp.concatenate([p_near_in[t - 1, j] for j in range(HALO)], axis=1)
            for i, (x, y) in enumerate(zip(halo_term(block_of(fp), oe, OWN), halo_term(hn, oe, ZN))):
                p_send[t - 1, 0, i] = fp[oe + HALO + i]
                p_send[t - 1, 1, i] = (fp[oe + HALO + i].astype(F32) + edge[i] - x - y).astype(BF16)
            to_other(2 * t, p_send.at[t - 1, 0], o0[t]).start()
            to_other(2 * t + 1, p_send.at[t - 1, 1], o1[t]).start()

    def complete(t, b, op, n):
        vals = jnp.concatenate([dinc[t - 1, i, q] for i in range(n) for q in range(Q)], axis=1)
        for j in range(HALO):
            b[j] = (b[j].astype(F32) - mm(vals, op[j])).astype(BF16)
    stores = []
    for t in range(T):
        inc, fa, fb = incs[t], f0[t], f1[t]
        near0, other0, near1, other1 = copies(t)
        crossing = has_o if t < DIAGONAL_FROM else plain_o
        if t == 0:
            for c in first:
                c.wait()
        else:
            @pl.when(has_p)
            def _(t=t):
                forward(t - 1).wait_recv()
        coupled = [mm(inc[q], coup_v[q]) for q in range(Q)]
        for n, r in enumerate(order):
            x = rhs_row(t, r).astype(F32)
            for q in range(Q):
                x = x - jnp.where(e[q] == r, coupled[q], 0.0)
            x = mm(x.astype(BF16), inv_v[r])
            g[r] = x
            fa[r + HALO] = x.astype(BF16)
            if n == 3 and t > 0:
                pl.when(crossing)(other0.start)
                near0.start()
        if t == 0:
            for c in tiles:
                c.wait()
            for r in order[:2]:
                operator_rows(r)
            pl.semaphore_wait(barrier, 1 + sum(there.astype(jnp.int32) for there, _ in greeted))
            near0.start()
            when_o(other0.start)
            when_o(lambda: y_copy().start())
        for i, x in enumerate(own(fa, oe)):
            part[oe + i] = x
        near0.wait_recv()
        hn = pair(n0[t])
        for i, x in enumerate(halo_term(hn, oe, ZN)):
            x = part[oe + i] - x
            part[oe + i] = x
            h1send[t, i] = x.astype(BF16)
        pl.when(crossing)(other1.start)
        if t == 0:
            mate_setup()
        if DIAGONAL_FROM <= t + 1 < T:
            seam_rows(t + 1)
        if t == 0:
            seam_operators()
        for p in order[2::2]:
            if t == 0:
                operator_rows(p)
                operator_rows(p + 1)
            for i, (x, y) in enumerate(zip(own(fa, p), halo_term(hn, p, ZN))):
                part[p + i] = x - y
        if t == 0:
            when_o(lambda: y_copy().wait_recv())
        mine = jnp.concatenate([fa[oe + HALO], fa[oe + HALO + 1]], axis=1)
        for i in range(HALO):
            ypart[i] = mm(mine, y_in[i])
        when_o(other0.wait_recv)
        if t >= DIAGONAL_FROM:
            @pl.when(seam)
            def _(t=t):
                if t == DIAGONAL_FROM:
                    for c in e_copies:
                        c.wait_recv()

                @pl.when(has_p)
                def _():
                    for i in range(2):
                        diagonal(t - 1, i).wait_recv()
                complete(t, o0[t], e0_in, 1)
        ho = pair(o0[t])
        for n, p in enumerate([ne, oe] + order[4::2]):
            for i, x in enumerate(halo_term(ho, p, ZO)):
                fb[p + i + HALO] = (part[p + i] - x).astype(BF16)
            if n == 0:
                near1.start()
        if t + 1 < T:
            x = mm(block_of(fb), rows_of(e[0], e[1], OWN))
            mid = [fb[e[q] + HALO].astype(F32) + g[e[q]] - x[:, q * W:(q + 1) * W] for q in range(Q)]
        else:
            for p in range(0, N, 2):
                for i, x in enumerate(own(fb, p)):
                    part[p + i] = x
        when_o(other1.wait_recv)
        if t >= DIAGONAL_FROM:
            @pl.when(seam)
            def _(t=t):
                complete(t, o1[t], e1_in, 2)
        near1.wait_recv()
        far = [(o1[t][i].astype(F32) - ypart[i]).astype(BF16) for i in range(HALO)]
        both = jnp.concatenate([n1[t][0], n1[t][1]] + far, axis=1)
        if t + 1 < T:
            x = mm(both, rows_of(e[0], e[1], HALOS))
            for q in range(Q):
                sent[t, q] = (mid[q] - x[:, q * W:(q + 1) * W]).astype(BF16)

            @pl.when(has_n)
            def _(t=t):
                forward(t).start()

            if t + 1 >= DIAGONAL_FROM:
                @pl.when(has_n & duo)
                def _(t=t):
                    diagonal(t, slot).start()
            for p in range(0, N, 2):
                for i, x in enumerate(own(fb, p)):
                    part[p + i] = x
        for p in range(0, N, 2):
            for i, x in enumerate(halo_term(both, p, HALOS)):
                out_v[t, :, (p + i) * W:(p + i + 1) * W] = (part[p + i] - x).astype(BF16)
            if p % 4 == 2:
                cut = slice((p - 2) * W, (p + 2) * W)
                c = pltpu.make_async_copy(out_v.at[t, :, cut], out.at[t, 0, :, cut], st.at[t, p // 4])
                c.start()
                stores.append(c)

    for t in range(T):
        near0, other0, near1, other1 = copies(t)
        near0.wait_send()
        near1.wait_send()
        when_o(other0.wait_send)
        when_o(other1.wait_send)
    when_o(lambda: y_copy().wait_send())
    for t in range(T - 1):
        @pl.when(has_n)
        def _(t=t):
            forward(t).wait_send()

        if t + 1 >= DIAGONAL_FROM:
            @pl.when(has_n & duo)
            def _(t=t):
                diagonal(t, slot).wait_send()

    @pl.when(seam)
    def _():
        for c in e_copies:
            c.wait_send()

    @pl.when(mate)
    def _():
        for c in mate_copies:
            c.wait_send()
    for c in stores:
        c.wait()


def on_device(S, FN, rhs, inflow, diag, off, cols, inv, coup, iface):
    T, _, M, _ = rhs.shape
    _, N, K, W, _ = off.shape
    Q = coup.shape[1]
    ANY = pl.BlockSpec(memory_space=pl.ANY)
    SM = pl.BlockSpec(memory_space=pltpu.SMEM)
    DMA = pltpu.SemaphoreType.DMA
    return pl.pallas_call(
        functools.partial(kernel, S, FN, T, N, K, Q, W),
        out_shape=jax.ShapeDtypeStruct(rhs.shape, BF16),
        in_specs=[SM, SM] + [ANY] * 6,
        out_specs=ANY,
        scratch_shapes=[
            pltpu.VMEM((T, M, N * W), BF16),
            pltpu.VMEM((N, W, W), BF16),
            pltpu.VMEM((N, K, W, W), BF16),
            pltpu.VMEM((N, W, W), BF16),
            pltpu.VMEM((Q, W, W), BF16),
            pltpu.VMEM((T, M, N * W), BF16),
            pltpu.VMEM((T - 1, Q, M, W), BF16),
        ]
        + [
            pltpu.VMEM((N, W, (N + 2 * HALO) * W), BF16),
            pltpu.VMEM((N, M, W), F32),
            pltpu.VMEM((HALO, M, W), F32),
            pltpu.VMEM((T, HALO, M, W), BF16),
            pltpu.VMEM((HALO, W, HALO * W), BF16),
            pltpu.VMEM((N, M, W), F32),
            pltpu.VMEM((N + 2 * HALO, M, W), BF16),
            pltpu.VMEM((T - 1, 2, HALO, M, W), BF16),
            pltpu.VMEM((T - 1, HALO, M, W), BF16),
            pltpu.VMEM((T - 1, HALO, M, W), BF16),
            pltpu.VMEM((HALO, W, Q * W), BF16),
            pltpu.VMEM((HALO, W, Q * W), BF16),
            pltpu.VMEM((HALO, W, Q * W), BF16),
            pltpu.VMEM((HALO, W, Q * W), BF16),
            pltpu.VMEM((HALO, W, 2 * Q * W), BF16),
            pltpu.VMEM((HALO, W, 2 * Q * W), BF16),
            pltpu.VMEM((T - 1, 2, Q, M, W), BF16),
        ]
        + [pltpu.VMEM((Q, M, W), BF16)] * T
        + [pltpu.VMEM((N + 2 * HALO, M, W), BF16)] * (2 * T)
        + [pltpu.VMEM((HALO, M, W), BF16)] * (4 * T)
        + [DMA((4 + Q + T,)), DMA((T, N // 4)), DMA((2 * T, 2)), DMA((2 * T, 2)), DMA((2,)), DMA((T - 1,)), DMA((T - 1,)), DMA((4,)), DMA((4,)), DMA((T - 1,)), DMA((T - 1, 2))],
        compiler_params=pltpu.CompilerParams(collective_id=0, has_side_effects=True, vmem_limit_bytes=48000000),
        name="sweep",
    )(*[pltpu.with_memory_space_constraint(x, pltpu.HBM) for x in (cols[0].T, iface, rhs, inflow, diag, off, inv, coup)])


def solution(mesh):
    placed = (
        P(None, "slab", None, "face"),
        P("slab", None, "face"),
        P("slab", "face", None, None),
        P("slab", "face", None, None, None),
        P("slab", "face", None),
        P("slab", "face", None, None),
        P("slab", "face", None, None),
        P("face"),
    )
    return jax.shard_map(
        functools.partial(on_device, mesh.shape["slab"], mesh.shape["face"]),
        mesh=mesh,
        in_specs=placed,
        out_specs=P(None, "slab", None, "face"),
        check_vma=False,
    )
```

```python
import functools

import jax
import jax.numpy as jnp
from jax import lax
from jax.experimental import pallas as pl
from jax.experimental.pallas import tpu as pltpu
from jax.sharding import PartitionSpec as P

HALO = 2
DIAGONAL_FROM = 1
MESH = pl.DeviceIdType.MESH
BF16 = jnp.bfloat16
F32 = jnp.float32


def mm(u, w):
    return lax.dot_general(u, w, (((1,), (1,)), ((), ())), preferred_element_type=F32)


def kernel(S, FN, T, N, K, Q, W, *refs):
    refs = list(refs)
    take = lambda n: [refs.pop(0) for _ in range(n)]
    cols_h, iface_h, rhs, inflow, diag, off, inv, coup = take(8)
    (out,) = take(1)
    rhs_v, diag_v, off_v, inv_v, coup_v, out_v, sent = take(7)
    z, part, ypart, h1send, y_in, g = take(6)
    fp, p_send, p_near, p_near_in, d_near, d_near_in, e0, e0_in, e1, e1_in, dinc = take(11)
    incs = take(T)
    f0, f1 = take(T), take(T)
    n0, o0, n1, o1 = take(T), take(T), take(T), take(T)
    ld, st, hs, hr, ysem, ssem, rsem, es, ps, ds, dr, cols, iface, ints = take(14)

    s = lax.axis_index("slab")
    f = lax.axis_index("face")
    odd = lax.rem(f, 2)
    has_o = (f > 0) & (f < FN - 1)
    has_p, has_n = s > 0, s < S - 1
    near = (s, f + 1 - 2 * odd)
    other = (s, jnp.clip(f - 1 + 2 * odd, 0, FN - 1))
    prev = (jnp.maximum(s - 1, 0), f)
    nxt = (jnp.minimum(s + 1, S - 1), f)
    SE = FN // 2
    seam = (f == SE - 1) | (f == SE)
    duo = (f >= SE - 2) & (f <= SE + 1)
    mate = duo & jnp.logical_not(seam)
    plain_o = has_o & jnp.logical_not(seam)
    across = jnp.where(f < SE, SE, SE - 1)
    slot = jnp.where(seam, 0, 1)
    oe = odd * (N - HALO)
    ne = (N - HALO) - oe
    o_slot = odd * (N + HALO)
    n_slot = (N + HALO) - o_slot

    barrier = pltpu.get_barrier_semaphore()
    pl.semaphore_signal(barrier, inc=1, device_id=near, device_id_type=MESH)
    greeted = ((has_o, other), (has_p, prev), (has_n, nxt), (duo & has_n, (nxt[0], across)), (seam & has_p, (prev[0], across)), (seam & has_p, (prev[0], jnp.where(f < SE, SE + 1, SE - 2))))
    for there, who in greeted:
        @pl.when(there)
        def _(who=who):
            pl.semaphore_signal(barrier, inc=1, device_id=who, device_id_type=MESH)

    index = [pltpu.make_async_copy(cols_h, cols, ints.at[0]), pltpu.make_async_copy(iface_h, iface, ints.at[1])]
    first = [
        pltpu.make_async_copy(inv.at[0], inv_v, ld.at[0]),
        pltpu.make_async_copy(rhs.at[0, 0], rhs_v.at[0], ld.at[1]),
        pltpu.make_async_copy(coup.at[0], coup_v, ld.at[2]),
    ]
    first += [pltpu.make_async_copy(inflow.at[0, :, q * W:(q + 1) * W], incs[0].at[q], ld.at[3 + q]) for q in range(Q)]
    tiles = [
        pltpu.make_async_copy(off.at[0], off_v, ld.at[3 + Q]),
        pltpu.make_async_copy(diag.at[0], diag_v, ld.at[4 + Q]),
    ]
    later = [pltpu.make_async_copy(rhs.at[t, 0], rhs_v.at[t], ld.at[4 + Q + t]) for t in range(1, T)]
    loads = index + first + tiles + later
    for c in loads:
        c.start()

    base = f * N - HALO

    def col(r, k):
        return jnp.clip(cols[k, r] - base, 0, N + 2 * HALO - 1)

    zero_halo = jnp.zeros((HALO,) + f0[0].shape[1:], BF16)
    for b in f0 + f1 + [fp]:
        b[0:HALO] = zero_halo
        b[N + HALO:N + 2 * HALO] = zero_halo

    @pl.when(jnp.logical_not(has_o))
    def _():
        for b in o0 + o1:
            b[...] = zero_halo
        y_in[...] = jnp.zeros(y_in.shape, BF16)

    @pl.when(s == 0)
    def _():
        for b in incs[1:]:
            b[...] = jnp.zeros(b.shape, BF16)

    @pl.when((s == 0) & seam)
    def _():
        dinc[...] = jnp.zeros(dinc.shape, BF16)

    for c in index:
        c.wait()
    e = [iface[q] for q in range(Q)]

    def to_near(i, src, dst):
        return pltpu.make_async_remote_copy(src_ref=src, dst_ref=dst, send_sem=hs.at[i, 0], recv_sem=hr.at[i, 0], device_id=near, device_id_type=MESH)

    def to_other(i, src, dst):
        return pltpu.make_async_remote_copy(src_ref=src, dst_ref=dst, send_sem=hs.at[i, 1], recv_sem=hr.at[i, 1], device_id=other, device_id_type=MESH)

    def copies(t):
        edge = lambda b, r: b.at[pl.ds(r + HALO, HALO)]
        return (
            to_near(2 * t, edge(f0[t], ne), n0[t]),
            to_other(2 * t, edge(f0[t], oe), o0[t]),
            to_near(2 * t + 1, edge(f1[t], ne), n1[t]),
            to_other(2 * t + 1, h1send.at[t], o1[t]),
        )

    def y_copy():
        return pltpu.make_async_remote_copy(src_ref=z.at[pl.ds(oe, HALO), :, (N + HALO) * W:(N + 2 * HALO) * W], dst_ref=y_in, send_sem=ysem.at[0], recv_sem=ysem.at[1], device_id=other, device_id_type=MESH)

    def forward(t):
        return pltpu.make_async_remote_copy(src_ref=sent.at[t], dst_ref=incs[t + 1], send_sem=ssem.at[t], recv_sem=rsem.at[t], device_id=nxt, device_id_type=MESH)

    def diagonal(t, i):
        return pltpu.make_async_remote_copy(src_ref=sent.at[t], dst_ref=dinc.at[t, i], send_sem=ds.at[t], recv_sem=dr.at[t, i], device_id=(nxt[0], across), device_id_type=MESH)

    def swap(src, dst, sems, i, dev):
        return pltpu.make_async_remote_copy(src_ref=src, dst_ref=dst, send_sem=sems.at[2 * i], recv_sem=sems.at[2 * i + 1], device_id=dev, device_id_type=MESH)

    e_copies = [swap(e0, e0_in, es, 0, other), swap(e1, e1_in, es, 1, other)]
    mate_copies = [swap(d_near, d_near_in, ps, 0, near), swap(p_near, p_near_in, ps, 1, near)]

    def when_o(act):
        @pl.when(has_o)
        def _():
            act()

    def operator_rows(r):
        prod = jnp.dot(inv_v[r], jnp.concatenate([diag_v[r]] + [off_v[r, k] for k in range(K)], axis=1), preferred_element_type=F32)
        prod = prod.astype(BF16)
        tiles = [prod[:, k * W:(k + 1) * W] for k in range(K + 1)]
        cs = [r + HALO] + [col(r, k) for k in range(K)]
        slots = [c + HALO for c in range(N)] + [n_slot + j for j in range(HALO)] + [o_slot + j for j in range(HALO)]
        for c, slot in enumerate(slots):
            x = None
            for k in range(0 if c < N else 1, K + 1):
                y = jnp.where(cs[k] == slot, tiles[k], jnp.zeros((), BF16))
                x = y if x is None else x + y
            z[r, :, c * W:(c + 1) * W] = x

    def block_of(b):
        return jnp.concatenate([b[c + HALO] for c in range(N)], axis=1)

    OWN, ZN, ZO = slice(0, N * W), slice(N * W, (N + HALO) * W), slice((N + HALO) * W, (N + 2 * HALO) * W)
    HALOS = slice(N * W, (N + 2 * HALO) * W)

    def own(b, p):
        return [b[p + i + HALO].astype(F32) + g[p + i] - x for i, x in enumerate(halo_term(block_of(b), p, OWN))]

    def rows_of(p, q, part_of):
        return jnp.concatenate([z[p, :, part_of], z[q, :, part_of]], axis=0)

    def halo_term(v, p, part_of):
        x = mm(v, z[pl.ds(p, 2), :, part_of].reshape(2 * W, v.shape[1]))
        return x[:, :W], x[:, W:]

    def pair(b):
        return jnp.concatenate([b[0], b[1]], axis=1)


    def nn(a, b):
        return jnp.dot(a, b, preferred_element_type=F32)

    order = [oe, oe + 1, ne, ne + 1] + list(range(HALO, N - HALO))

    def rhs_row(t, r):
        return rhs_v[t, :, pl.ds(pl.multiple_of(r * W, W), W)]

    d = []

    def placed(r):
        return jnp.concatenate([jnp.where(e[q] == r, d[q].astype(F32), 0.0) for q in range(Q)], axis=1)

    def mate_setup():
        d.extend(nn(inv_v[e[q]], coup_v[q]).astype(BF16) for q in range(Q))

        @pl.when(mate)
        def _():
            for j in range(HALO):
                d_near[j] = placed(ne + j).astype(BF16)
            mate_copies[0].start()
            for t in range(1, T):
                later[t - 1].wait()
                for j in range(HALO):
                    p_near[t - 1, j] = mm(rhs_row(t, ne + j), inv_v[ne + j]).astype(BF16)
            mate_copies[1].start()

        @pl.when(jnp.logical_not(mate))
        def _():
            for c in later:
                c.wait()

    def own_tile(r, c):
        x = jnp.zeros((W, W), BF16)
        for j in range(N):
            x = x + jnp.where(c == j, z[r, :, j * W:(j + 1) * W], jnp.zeros((), BF16))
        return x

    def seam_operators():
        @pl.when(seam)
        def _():
            mate_copies[0].wait_recv()
            below = jnp.concatenate([d_near_in[j] for j in range(HALO)], axis=0)
            for i in range(HALO):
                r = oe + i
                d_r = placed(r)
                e0[i] = d_r.astype(BF16)
                mine = jnp.concatenate([nn(own_tile(r, e[q]), d[q]) for q in range(Q)], axis=1)
                e1[i, :, 0:Q * W] = (2.0 * d_r - mine).astype(BF16)
                e1[i, :, Q * W:2 * Q * W] = (-nn(z[r, :, ZN], below)).astype(BF16)
            for c in e_copies:
                c.start()

    def seam_rows(t):
        @pl.when(seam)
        def _():
            if t == DIAGONAL_FROM:
                mate_copies[1].wait_recv()
            edge = []
            for r in order:
                x = mm(rhs_row(t, r), inv_v[r])
                fp[r + HALO] = x.astype(BF16)
                if len(edge) < HALO:
                    edge.append(x)
            hn = jnp.concatenate([p_near_in[t - 1, j] for j in range(HALO)], axis=1)
            for i, (x, y) in enumerate(zip(halo_term(block_of(fp), oe, OWN), halo_term(hn, oe, ZN))):
                p_send[t - 1, 0, i] = fp[oe + HALO + i]
                p_send[t - 1, 1, i] = (fp[oe + HALO + i].astype(F32) + edge[i] - x - y).astype(BF16)
            to_other(2 * t, p_send.at[t - 1, 0], o0[t]).start()
            to_other(2 * t + 1, p_send.at[t - 1, 1], o1[t]).start()

    def complete(t, b, op, n):
        vals = jnp.concatenate([dinc[t - 1, i, q] for i in range(n) for q in range(Q)], axis=1)
        for j in range(HALO):
            b[j] = (b[j].astype(F32) - mm(vals, op[j])).astype(BF16)
    stores = []
    for t in range(T):
        inc, fa, fb = incs[t], f0[t], f1[t]
        near0, other0, near1, other1 = copies(t)
        crossing = has_o if t < DIAGONAL_FROM else plain_o
        if t == 0:
            for c in first:
                c.wait()
        else:
            @pl.when(has_p)
            def _(t=t):
                forward(t - 1).wait_recv()
        coupled = [mm(inc[q], coup_v[q]) for q in range(Q)]
        for n, r in enumerate(order):
            x = rhs_row(t, r).astype(F32)
            for q in range(Q):
                x = x - jnp.where(e[q] == r, coupled[q], 0.0)
            x = mm(x.astype(BF16), inv_v[r])
            g[r] = x
            fa[r + HALO] = x.astype(BF16)
            if n == 3:
                if t == 0:
                    pl.semaphore_wait(barrier, 1 + sum(there.astype(jnp.int32) for there, _ in greeted))
                pl.when(crossing)(other0.start)
                near0.start()
        if t == 0:
            for c in tiles:
                c.wait()
            for r in order[:2]:
                operator_rows(r)
            when_o(lambda: y_copy().start())
        for i, x in enumerate(own(fa, oe)):
            part[oe + i] = x
        near0.wait_recv()
        hn = pair(n0[t])
        for i, x in enumerate(halo_term(hn, oe, ZN)):
            x = part[oe + i] - x
            part[oe + i] = x
            h1send[t, i] = x.astype(BF16)
        pl.when(crossing)(other1.start)
        if t == 0:
            mate_setup()
        if DIAGONAL_FROM <= t + 1 < T:
            seam_rows(t + 1)
        if t == 0:
            seam_operators()
        for p in order[2::2]:
            if t == 0:
                operator_rows(p)
                operator_rows(p + 1)
            for i, (x, y) in enumerate(zip(own(fa, p), halo_term(hn, p, ZN))):
                part[p + i] = x - y
        if t == 0:
            when_o(lambda: y_copy().wait_recv())
        mine = jnp.concatenate([fa[oe + HALO], fa[oe + HALO + 1]], axis=1)
        for i in range(HALO):
            ypart[i] = mm(mine, y_in[i])
        when_o(other0.wait_recv)
        if t >= DIAGONAL_FROM:
            @pl.when(seam)
            def _(t=t):
                if t == DIAGONAL_FROM:
                    for c in e_copies:
                        c.wait_recv()

                @pl.when(has_p)
                def _():
                    for i in range(2):
                        diagonal(t - 1, i).wait_recv()
                complete(t, o0[t], e0_in, 1)
        ho = pair(o0[t])
        for n, p in enumerate([ne, oe] + order[4::2]):
            for i, x in enumerate(halo_term(ho, p, ZO)):
                fb[p + i + HALO] = (part[p + i] - x).astype(BF16)
            if n == 0:
                near1.start()
        if t + 1 < T:
            x = mm(block_of(fb), rows_of(e[0], e[1], OWN))
            mid = [fb[e[q] + HALO].astype(F32) + g[e[q]] - x[:, q * W:(q + 1) * W] for q in range(Q)]
        else:
            for p in range(0, N, 2):
                for i, x in enumerate(own(fb, p)):
                    part[p + i] = x
        when_o(other1.wait_recv)
        if t >= DIAGONAL_FROM:
            @pl.when(seam)
            def _(t=t):
                complete(t, o1[t], e1_in, 2)
        near1.wait_recv()
        far = [(o1[t][i].astype(F32) - ypart[i]).astype(BF16) for i in range(HALO)]
        both = jnp.concatenate([n1[t][0], n1[t][1]] + far, axis=1)
        if t + 1 < T:
            x = mm(both, rows_of(e[0], e[1], HALOS))
            for q in range(Q):
                sent[t, q] = (mid[q] - x[:, q * W:(q + 1) * W]).astype(BF16)

            @pl.when(has_n)
            def _(t=t):
                forward(t).start()

            if t + 1 >= DIAGONAL_FROM:
                @pl.when(has_n & duo)
                def _(t=t):
                    diagonal(t, slot).start()
            for p in range(0, N, 2):
                for i, x in enumerate(own(fb, p)):
                    part[p + i] = x
        for p in range(0, N, 2):
            for i, x in enumerate(halo_term(both, p, HALOS)):
                out_v[t, :, (p + i) * W:(p + i + 1) * W] = (part[p + i] - x).astype(BF16)
            if p % 4 == 2:
                cut = slice((p - 2) * W, (p + 2) * W)
                c = pltpu.make_async_copy(out_v.at[t, :, cut], out.at[t, 0, :, cut], st.at[t, p // 4])
                c.start()
                stores.append(c)

    for t in range(T):
        near0, other0, near1, other1 = copies(t)
        near0.wait_send()
        near1.wait_send()
        when_o(other0.wait_send)
        when_o(other1.wait_send)
    when_o(lambda: y_copy().wait_send())
    for t in range(T - 1):
        @pl.when(has_n)
        def _(t=t):
            forward(t).wait_send()

        if t + 1 >= DIAGONAL_FROM:
            @pl.when(has_n & duo)
            def _(t=t):
                diagonal(t, slot).wait_send()

    @pl.when(seam)
    def _():
        for c in e_copies:
            c.wait_send()

    @pl.when(mate)
    def _():
        for c in mate_copies:
            c.wait_send()
    for c in stores:
        c.wait()


def on_device(S, FN, rhs, inflow, diag, off, cols, inv, coup, iface):
    T, _, M, _ = rhs.shape
    _, N, K, W, _ = off.shape
    Q = coup.shape[1]
    ANY = pl.BlockSpec(memory_space=pl.ANY)
    DMA = pltpu.SemaphoreType.DMA
    return pl.pallas_call(
        functools.partial(kernel, S, FN, T, N, K, Q, W),
        out_shape=jax.ShapeDtypeStruct(rhs.shape, BF16),
        in_specs=[ANY] * 8,
        out_specs=ANY,
        scratch_shapes=[
            pltpu.VMEM((T, M, N * W), BF16),
            pltpu.VMEM((N, W, W), BF16),
            pltpu.VMEM((N, K, W, W), BF16),
            pltpu.VMEM((N, W, W), BF16),
            pltpu.VMEM((Q, W, W), BF16),
            pltpu.VMEM((T, M, N * W), BF16),
            pltpu.VMEM((T - 1, Q, M, W), BF16),
        ]
        + [
            pltpu.VMEM((N, W, (N + 2 * HALO) * W), BF16),
            pltpu.VMEM((N, M, W), F32),
            pltpu.VMEM((HALO, M, W), F32),
            pltpu.VMEM((T, HALO, M, W), BF16),
            pltpu.VMEM((HALO, W, HALO * W), BF16),
            pltpu.VMEM((N, M, W), F32),
            pltpu.VMEM((N + 2 * HALO, M, W), BF16),
            pltpu.VMEM((T - 1, 2, HALO, M, W), BF16),
            pltpu.VMEM((T - 1, HALO, M, W), BF16),
            pltpu.VMEM((T - 1, HALO, M, W), BF16),
            pltpu.VMEM((HALO, W, Q * W), BF16),
            pltpu.VMEM((HALO, W, Q * W), BF16),
            pltpu.VMEM((HALO, W, Q * W), BF16),
            pltpu.VMEM((HALO, W, Q * W), BF16),
            pltpu.VMEM((HALO, W, 2 * Q * W), BF16),
            pltpu.VMEM((HALO, W, 2 * Q * W), BF16),
            pltpu.VMEM((T - 1, 2, Q, M, W), BF16),
        ]
        + [pltpu.VMEM((Q, M, W), BF16)] * T
        + [pltpu.VMEM((N + 2 * HALO, M, W), BF16)] * (2 * T)
        + [pltpu.VMEM((HALO, M, W), BF16)] * (4 * T)
        + [DMA((4 + Q + T,)), DMA((T, N // 4)), DMA((2 * T, 2)), DMA((2 * T, 2)), DMA((2,)), DMA((T - 1,)), DMA((T - 1,)), DMA((4,)), DMA((4,)), DMA((T - 1,)), DMA((T - 1, 2)), pltpu.SMEM((K, N), jnp.int32), pltpu.SMEM((Q,), jnp.int32), DMA((2,))],
        compiler_params=pltpu.CompilerParams(collective_id=0, has_side_effects=True, vmem_limit_bytes=48000000),
        name="sweep",
    )(*[pltpu.with_memory_space_constraint(x, pltpu.HBM) for x in (cols[0].T, iface, rhs, inflow, diag, off, inv, coup)])


def solution(mesh):
    placed = (
        P(None, "slab", None, "face"),
        P("slab", None, "face"),
        P("slab", "face", None, None),
        P("slab", "face", None, None, None),
        P("slab", "face", None),
        P("slab", "face", None, None),
        P("slab", "face", None, None),
        P("face"),
    )
    return jax.shard_map(
        functools.partial(on_device, mesh.shape["slab"], mesh.shape["face"]),
        mesh=mesh,
        in_specs=placed,
        out_specs=P(None, "slab", None, "face"),
        check_vma=False,
    )
```

```python
import functools

import jax
import jax.numpy as jnp
from jax import lax
from jax.experimental import pallas as pl
from jax.experimental.pallas import tpu as pltpu
from jax.sharding import PartitionSpec as P

HALO = 2
DIAGONAL_FROM = 1
MESH = pl.DeviceIdType.MESH
BF16 = jnp.bfloat16
F32 = jnp.float32


def mm(u, w):
    return lax.dot_general(u, w, (((1,), (1,)), ((), ())), preferred_element_type=F32)


def kernel(S, FN, T, N, K, Q, W, *refs):
    refs = list(refs)
    take = lambda n: [refs.pop(0) for _ in range(n)]
    cols_h, iface_h, rhs, inflow, diag, off, inv, coup = take(8)
    (out,) = take(1)
    rhs_v, diag_v, off_v, inv_v, coup_v, out_v, sent = take(7)
    z, part, ypart, h1send, y_in, g = take(6)
    fp, p_send, p_near, p_near_in, d_near, d_near_in, e0, e0_in, e1, e1_in, dinc = take(11)
    incs = take(T)
    f0, f1 = take(T), take(T)
    n0, o0, n1, o1 = take(T), take(T), take(T), take(T)
    ld, st, hs, hr, ysem, ssem, rsem, es, ps, ds, dr, cols, iface, ints = take(14)

    s = lax.axis_index("slab")
    f = lax.axis_index("face")
    odd = lax.rem(f, 2)
    has_o = (f > 0) & (f < FN - 1)
    has_p, has_n = s > 0, s < S - 1
    near = (s, f + 1 - 2 * odd)
    other = (s, jnp.clip(f - 1 + 2 * odd, 0, FN - 1))
    prev = (jnp.maximum(s - 1, 0), f)
    nxt = (jnp.minimum(s + 1, S - 1), f)
    SE = FN // 2
    seam = (f == SE - 1) | (f == SE)
    duo = (f >= SE - 2) & (f <= SE + 1)
    mate = duo & jnp.logical_not(seam)
    plain_o = has_o & jnp.logical_not(seam)
    across = jnp.where(f < SE, SE, SE - 1)
    slot = jnp.where(seam, 0, 1)
    oe = odd * (N - HALO)
    ne = (N - HALO) - oe
    o_slot = odd * (N + HALO)
    n_slot = (N + HALO) - o_slot

    barrier = pltpu.get_barrier_semaphore()
    pl.semaphore_signal(barrier, inc=1, device_id=near, device_id_type=MESH)
    greeted = ((has_o, other), (has_p, prev), (has_n, nxt), (duo & has_n, (nxt[0], across)), (seam & has_p, (prev[0], across)), (seam & has_p, (prev[0], jnp.where(f < SE, SE + 1, SE - 2))))
    for there, who in greeted:
        @pl.when(there)
        def _(who=who):
            pl.semaphore_signal(barrier, inc=1, device_id=who, device_id_type=MESH)

    index = [pltpu.make_async_copy(cols_h, cols, ints.at[0]), pltpu.make_async_copy(iface_h, iface, ints.at[1])]
    first = [
        pltpu.make_async_copy(inv.at[0], inv_v, ld.at[0]),
        pltpu.make_async_copy(rhs.at[0, 0], rhs_v.at[0], ld.at[1]),
        pltpu.make_async_copy(coup.at[0], coup_v, ld.at[2]),
    ]
    first += [pltpu.make_async_copy(inflow.at[0, :, q * W:(q + 1) * W], incs[0].at[q], ld.at[3 + q]) for q in range(Q)]
    tiles = [
        pltpu.make_async_copy(off.at[0], off_v, ld.at[3 + Q]),
        pltpu.make_async_copy(diag.at[0], diag_v, ld.at[4 + Q]),
    ]
    later = [pltpu.make_async_copy(rhs.at[t, 0], rhs_v.at[t], ld.at[4 + Q + t]) for t in range(1, T)]
    loads = index + first + tiles + later
    for c in loads:
        c.start()

    base = f * N - HALO

    def col(r, k):
        return jnp.clip(cols[k, r] - base, 0, N + 2 * HALO - 1)

    zero_halo = jnp.zeros((HALO,) + f0[0].shape[1:], BF16)
    for b in f0 + f1 + [fp]:
        b[0:HALO] = zero_halo
        b[N + HALO:N + 2 * HALO] = zero_halo

    @pl.when(jnp.logical_not(has_o))
    def _():
        for b in o0 + o1:
            b[...] = zero_halo
        y_in[...] = jnp.zeros(y_in.shape, BF16)

    @pl.when(s == 0)
    def _():
        for b in incs[1:]:
            b[...] = jnp.zeros(b.shape, BF16)

    @pl.when((s == 0) & seam)
    def _():
        dinc[...] = jnp.zeros(dinc.shape, BF16)

    for c in index:
        c.wait()
    e = [jnp.clip(iface[q], 0, N - 1) for q in range(Q)]

    def to_near(i, src, dst):
        return pltpu.make_async_remote_copy(src_ref=src, dst_ref=dst, send_sem=hs.at[i, 0], recv_sem=hr.at[i, 0], device_id=near, device_id_type=MESH)

    def to_other(i, src, dst):
        return pltpu.make_async_remote_copy(src_ref=src, dst_ref=dst, send_sem=hs.at[i, 1], recv_sem=hr.at[i, 1], device_id=other, device_id_type=MESH)

    def copies(t):
        edge = lambda b, r: b.at[pl.ds(r + HALO, HALO)]
        return (
            to_near(2 * t, edge(f0[t], ne), n0[t]),
            to_other(2 * t, edge(f0[t], oe), o0[t]),
            to_near(2 * t + 1, edge(f1[t], ne), n1[t]),
            to_other(2 * t + 1, h1send.at[t], o1[t]),
        )

    def y_copy():
        return pltpu.make_async_remote_copy(src_ref=z.at[pl.ds(oe, HALO), :, (N + HALO) * W:(N + 2 * HALO) * W], dst_ref=y_in, send_sem=ysem.at[0], recv_sem=ysem.at[1], device_id=other, device_id_type=MESH)

    def forward(t):
        return pltpu.make_async_remote_copy(src_ref=sent.at[t], dst_ref=incs[t + 1], send_sem=ssem.at[t], recv_sem=rsem.at[t], device_id=nxt, device_id_type=MESH)

    def diagonal(t, i):
        return pltpu.make_async_remote_copy(src_ref=sent.at[t], dst_ref=dinc.at[t, i], send_sem=ds.at[t], recv_sem=dr.at[t, i], device_id=(nxt[0], across), device_id_type=MESH)

    def swap(src, dst, sems, i, dev):
        return pltpu.make_async_remote_copy(src_ref=src, dst_ref=dst, send_sem=sems.at[2 * i], recv_sem=sems.at[2 * i + 1], device_id=dev, device_id_type=MESH)

    e_copies = [swap(e0, e0_in, es, 0, other), swap(e1, e1_in, es, 1, other)]
    mate_copies = [swap(d_near, d_near_in, ps, 0, near), swap(p_near, p_near_in, ps, 1, near)]

    def when_o(act):
        @pl.when(has_o)
        def _():
            act()

    def operator_rows(r):
        prod = jnp.dot(inv_v[r], jnp.concatenate([diag_v[r]] + [off_v[r, k] for k in range(K)], axis=1), preferred_element_type=F32)
        prod = prod.astype(BF16)
        tiles = [prod[:, k * W:(k + 1) * W] for k in range(K + 1)]
        cs = [r + HALO] + [col(r, k) for k in range(K)]
        slots = [c + HALO for c in range(N)] + [n_slot + j for j in range(HALO)] + [o_slot + j for j in range(HALO)]
        for c, slot in enumerate(slots):
            x = None
            for k in range(0 if c < N else 1, K + 1):
                y = jnp.where(cs[k] == slot, tiles[k], jnp.zeros((), BF16))
                x = y if x is None else x + y
            z[r, :, c * W:(c + 1) * W] = x

    def block_of(b):
        return jnp.concatenate([b[c + HALO] for c in range(N)], axis=1)

    OWN, ZN, ZO = slice(0, N * W), slice(N * W, (N + HALO) * W), slice((N + HALO) * W, (N + 2 * HALO) * W)
    HALOS = slice(N * W, (N + 2 * HALO) * W)

    def own(b, p):
        return [b[p + i + HALO].astype(F32) + g[p + i] - x for i, x in enumerate(halo_term(block_of(b), p, OWN))]

    def rows_of(p, q, part_of):
        return jnp.concatenate([z[p, :, part_of], z[q, :, part_of]], axis=0)

    def halo_term(v, p, part_of):
        x = mm(v, z[pl.ds(p, 2), :, part_of].reshape(2 * W, v.shape[1]))
        return x[:, :W], x[:, W:]

    def pair(b):
        return jnp.concatenate([b[0], b[1]], axis=1)


    def nn(a, b):
        return jnp.dot(a, b, preferred_element_type=F32)

    order = [oe, oe + 1, ne, ne + 1] + list(range(HALO, N - HALO))

    def rhs_row(t, r):
        return rhs_v[t, :, pl.ds(pl.multiple_of(r * W, W), W)]

    d = []

    def placed(r):
        return jnp.concatenate([jnp.where(e[q] == r, d[q].astype(F32), 0.0) for q in range(Q)], axis=1)

    def mate_setup():
        d.extend(nn(inv_v[e[q]], coup_v[q]).astype(BF16) for q in range(Q))

        @pl.when(mate)
        def _():
            for j in range(HALO):
                d_near[j] = placed(ne + j).astype(BF16)
            mate_copies[0].start()
            for t in range(1, T):
                later[t - 1].wait()
                for j in range(HALO):
                    p_near[t - 1, j] = mm(rhs_row(t, ne + j), inv_v[ne + j]).astype(BF16)
            mate_copies[1].start()

        @pl.when(jnp.logical_not(mate))
        def _():
            for c in later:
                c.wait()

    def own_tile(r, c):
        x = jnp.zeros((W, W), BF16)
        for j in range(N):
            x = x + jnp.where(c == j, z[r, :, j * W:(j + 1) * W], jnp.zeros((), BF16))
        return x

    def seam_operators():
        @pl.when(seam)
        def _():
            mate_copies[0].wait_recv()
            below = jnp.concatenate([d_near_in[j] for j in range(HALO)], axis=0)
            for i in range(HALO):
                r = oe + i
                d_r = placed(r)
                e0[i] = d_r.astype(BF16)
                mine = jnp.concatenate([nn(own_tile(r, e[q]), d[q]) for q in range(Q)], axis=1)
                e1[i, :, 0:Q * W] = (2.0 * d_r - mine).astype(BF16)
                e1[i, :, Q * W:2 * Q * W] = (-nn(z[r, :, ZN], below)).astype(BF16)
            for c in e_copies:
                c.start()

    def seam_rows(t):
        @pl.when(seam)
        def _():
            if t == DIAGONAL_FROM:
                mate_copies[1].wait_recv()
            edge = []
            for r in order:
                x = mm(rhs_row(t, r), inv_v[r])
                fp[r + HALO] = x.astype(BF16)
                if len(edge) < HALO:
                    edge.append(x)
            hn = jnp.concatenate([p_near_in[t - 1, j] for j in range(HALO)], axis=1)
            for i, (x, y) in enumerate(zip(halo_term(block_of(fp), oe, OWN), halo_term(hn, oe, ZN))):
                p_send[t - 1, 0, i] = fp[oe + HALO + i]
                p_send[t - 1, 1, i] = (fp[oe + HALO + i].astype(F32) + edge[i] - x - y).astype(BF16)
            to_other(2 * t, p_send.at[t - 1, 0], o0[t]).start()
            to_other(2 * t + 1, p_send.at[t - 1, 1], o1[t]).start()

    def complete(t, b, op, n):
        vals = jnp.concatenate([dinc[t - 1, i, q] for i in range(n) for q in range(Q)], axis=1)
        for j in range(HALO):
            b[j] = (b[j].astype(F32) - mm(vals, op[j])).astype(BF16)
    stores = []
    for t in range(T):
        inc, fa, fb = incs[t], f0[t], f1[t]
        near0, other0, near1, other1 = copies(t)
        crossing = has_o if t < DIAGONAL_FROM else plain_o
        if t == 0:
            for c in first:
                c.wait()
        else:
            @pl.when(has_p)
            def _(t=t):
                forward(t - 1).wait_recv()
        coupled = [mm(inc[q], coup_v[q]) for q in range(Q)]
        for n, r in enumerate(order):
            x = rhs_row(t, r).astype(F32)
            for q in range(Q):
                x = x - jnp.where(e[q] == r, coupled[q], 0.0)
            x = mm(x.astype(BF16), inv_v[r])
            g[r] = x
            fa[r + HALO] = x.astype(BF16)
            if n == (3 if t == 0 else 1):
                if t == 0:
                    pl.semaphore_wait(barrier, 1 + sum(there.astype(jnp.int32) for there, _ in greeted))
                pl.when(crossing)(other0.start)
            if n == 3:
                near0.start()
        if t == 0:
            for c in tiles:
                c.wait()
            for r in order[:2]:
                operator_rows(r)
            when_o(lambda: y_copy().start())
        for i, x in enumerate(own(fa, oe)):
            part[oe + i] = x
        if t > 0 and DIAGONAL_FROM <= t + 1 < T:
            seam_rows(t + 1)
        near0.wait_recv()
        hn = pair(n0[t])
        for i, x in enumerate(halo_term(hn, oe, ZN)):
            x = part[oe + i] - x
            part[oe + i] = x
            h1send[t, i] = x.astype(BF16)
        pl.when(crossing)(other1.start)
        if t == 0:
            mate_setup()
            if DIAGONAL_FROM == 1:
                seam_rows(1)
            seam_operators()
        for p in order[2::2]:
            if t == 0:
                operator_rows(p)
                operator_rows(p + 1)
            for i, (x, y) in enumerate(zip(own(fa, p), halo_term(hn, p, ZN))):
                part[p + i] = x - y
        if t == 0:
            when_o(lambda: y_copy().wait_recv())
        mine = jnp.concatenate([fa[oe + HALO], fa[oe + HALO + 1]], axis=1)
        for i in range(HALO):
            ypart[i] = mm(mine, y_in[i])
        when_o(other0.wait_recv)
        if t >= DIAGONAL_FROM:
            @pl.when(seam)
            def _(t=t):
                if t == DIAGONAL_FROM:
                    for c in e_copies:
                        c.wait_recv()

                @pl.when(has_p)
                def _():
                    for i in range(2):
                        diagonal(t - 1, i).wait_recv()
                complete(t, o0[t], e0_in, 1)
        ho = pair(o0[t])
        for n, p in enumerate([ne, oe] + order[4::2]):
            for i, x in enumerate(halo_term(ho, p, ZO)):
                fb[p + i + HALO] = (part[p + i] - x).astype(BF16)
            if n == 0:
                near1.start()
        if t + 1 < T:
            x = mm(block_of(fb), rows_of(e[0], e[1], OWN))
            mid = [fb[e[q] + HALO].astype(F32) + g[e[q]] - x[:, q * W:(q + 1) * W] for q in range(Q)]
        else:
            for p in range(0, N, 2):
                for i, x in enumerate(own(fb, p)):
                    part[p + i] = x
        when_o(other1.wait_recv)
        if t >= DIAGONAL_FROM:
            @pl.when(seam)
            def _(t=t):
                complete(t, o1[t], e1_in, 2)
        far = [(o1[t][i].astype(F32) - ypart[i]).astype(BF16) for i in range(HALO)]
        far = jnp.concatenate(far, axis=1)
        if t + 1 < T:
            x = mm(far, rows_of(e[0], e[1], ZO))
            mid = [mid[q] - x[:, q * W:(q + 1) * W] for q in range(Q)]
        else:
            for p in range(0, N, 2):
                for i, x in enumerate(halo_term(far, p, ZO)):
                    part[p + i] = part[p + i] - x
        near1.wait_recv()
        hn = pair(n1[t])
        if t + 1 < T:
            x = mm(hn, rows_of(e[0], e[1], ZN))
            for q in range(Q):
                sent[t, q] = (mid[q] - x[:, q * W:(q + 1) * W]).astype(BF16)

            @pl.when(has_n)
            def _(t=t):
                forward(t).start()

            if t + 1 >= DIAGONAL_FROM:
                @pl.when(has_n & duo)
                def _(t=t):
                    diagonal(t, slot).start()
            for p in range(0, N, 2):
                for i, x in enumerate(own(fb, p)):
                    part[p + i] = x
        for p in range(0, N, 2):
            last = t + 1 == T
            vals = hn if last else jnp.concatenate([hn, far], axis=1)
            for i, x in enumerate(halo_term(vals, p, ZN if last else HALOS)):
                out_v[t, :, (p + i) * W:(p + i + 1) * W] = (part[p + i] - x).astype(BF16)
            if p % 4 == 2:
                cut = slice((p - 2) * W, (p + 2) * W)
                c = pltpu.make_async_copy(out_v.at[t, :, cut], out.at[t, 0, :, cut], st.at[t, p // 4])
                c.start()
                stores.append(c)

    for t in range(T):
        near0, other0, near1, other1 = copies(t)
        near0.wait_send()
        near1.wait_send()
        when_o(other0.wait_send)
        when_o(other1.wait_send)
    when_o(lambda: y_copy().wait_send())
    for t in range(T - 1):
        @pl.when(has_n)
        def _(t=t):
            forward(t).wait_send()

        if t + 1 >= DIAGONAL_FROM:
            @pl.when(has_n & duo)
            def _(t=t):
                diagonal(t, slot).wait_send()

    @pl.when(seam)
    def _():
        for c in e_copies:
            c.wait_send()

    @pl.when(mate)
    def _():
        for c in mate_copies:
            c.wait_send()
    for c in stores:
        c.wait()


def on_device(S, FN, rhs, inflow, diag, off, cols, inv, coup, iface):
    T, _, M, _ = rhs.shape
    _, N, K, W, _ = off.shape
    Q = coup.shape[1]
    ANY = pl.BlockSpec(memory_space=pl.ANY)
    DMA = pltpu.SemaphoreType.DMA
    return pl.pallas_call(
        functools.partial(kernel, S, FN, T, N, K, Q, W),
        out_shape=jax.ShapeDtypeStruct(rhs.shape, BF16),
        in_specs=[ANY] * 8,
        out_specs=ANY,
        scratch_shapes=[
            pltpu.VMEM((T, M, N * W), BF16),
            pltpu.VMEM((N, W, W), BF16),
            pltpu.VMEM((N, K, W, W), BF16),
            pltpu.VMEM((N, W, W), BF16),
            pltpu.VMEM((Q, W, W), BF16),
            pltpu.VMEM((T, M, N * W), BF16),
            pltpu.VMEM((T - 1, Q, M, W), BF16),
        ]
        + [
            pltpu.VMEM((N, W, (N + 2 * HALO) * W), BF16),
            pltpu.VMEM((N, M, W), F32),
            pltpu.VMEM((HALO, M, W), F32),
            pltpu.VMEM((T, HALO, M, W), BF16),
            pltpu.VMEM((HALO, W, HALO * W), BF16),
            pltpu.VMEM((N, M, W), F32),
            pltpu.VMEM((N + 2 * HALO, M, W), BF16),
            pltpu.VMEM((T - 1, 2, HALO, M, W), BF16),
            pltpu.VMEM((T - 1, HALO, M, W), BF16),
            pltpu.VMEM((T - 1, HALO, M, W), BF16),
            pltpu.VMEM((HALO, W, Q * W), BF16),
            pltpu.VMEM((HALO, W, Q * W), BF16),
            pltpu.VMEM((HALO, W, Q * W), BF16),
            pltpu.VMEM((HALO, W, Q * W), BF16),
            pltpu.VMEM((HALO, W, 2 * Q * W), BF16),
            pltpu.VMEM((HALO, W, 2 * Q * W), BF16),
            pltpu.VMEM((T - 1, 2, Q, M, W), BF16),
        ]
        + [pltpu.VMEM((Q, M, W), BF16)] * T
        + [pltpu.VMEM((N + 2 * HALO, M, W), BF16)] * (2 * T)
        + [pltpu.VMEM((HALO, M, W), BF16)] * (4 * T)
        + [DMA((4 + Q + T,)), DMA((T, N // 4)), DMA((2 * T, 2)), DMA((2 * T, 2)), DMA((2,)), DMA((T - 1,)), DMA((T - 1,)), DMA((4,)), DMA((4,)), DMA((T - 1,)), DMA((T - 1, 2)), pltpu.SMEM((K, N), jnp.int32), pltpu.SMEM((Q,), jnp.int32), DMA((2,))],
        compiler_params=pltpu.CompilerParams(collective_id=0, has_side_effects=True, vmem_limit_bytes=48000000),
        name="sweep",
    )(*[pltpu.with_memory_space_constraint(x, pltpu.HBM) for x in (cols[0].T, iface, rhs, inflow, diag, off, inv, coup)])


def solution(mesh):
    placed = (
        P(None, "slab", None, "face"),
        P("slab", None, "face"),
        P("slab", "face", None, None),
        P("slab", "face", None, None, None),
        P("slab", "face", None),
        P("slab", "face", None, None),
        P("slab", "face", None, None),
        P("face"),
    )
    return jax.shard_map(
        functools.partial(on_device, mesh.shape["slab"], mesh.shape["face"]),
        mesh=mesh,
        in_specs=placed,
        out_specs=P(None, "slab", None, "face"),
        check_vma=False,
    )
```
